32 devices in a mesh: depth: 4 (over y, x), tile: 8 (over z, core).
Axes of the slice: x: 2, y: 2, z: 4, core: 2. Of those that a mesh axis runs over, the one named last changes fastest.
Arguments:
- density: bfloat16 [128, 512, 2048], P('depth', 'tile'), may hold values from 0 to 2
- depth_rank: int32 [4], replicated, may hold values from 0 to 3, as said below
- piece_home: int32 [64], P('tile'), may hold values from 0 to 63, as said below
Outputs:
- display: float32 [3, 4, 64, 4096], P(None, 'depth', 'tile')
The draws below stay inside these ranges and needn't reach their ends.
Inputs may be any that keep to these rules, and one draw needn't show every extreme that they name: Either depth_rank[i] = i for every i, or depth_rank[i] = 3 - i for every i. `piece_home`: every value appears exactly once. A value h names slot h % 8 of the device h // 8 along tile. The number of the 8 entries of tile device s that name device o depends only on (o - s) mod 8, is at most 2, and equals 2 for some pair.
All inputs are finite; a program needn't handle non-finite values.
Results may differ from the reference program's by a relative error of at most 0.0003.
Values may be sent and summed in bfloat16 or wider, within the bound.
A program may use at most 128 MiB of HBM per device.

```python
import math
from functools import partial
import jax
import jax.numpy as jnp
from jax import lax

CZ = 32
BY = 64
IMAGE_COLUMNS = 2048
VIEW_CELLS = 128
IMAGE_ROWS = 512
PPD = 8
PR = 4096
PIECES = 64
N_DEPTH = 4
N_TILE = 8


def draw_density(key, part):
    random_keys = jax.random.split(key, 4)
    low_end, high_end = (0.003, 0.25)
    logs = jax.random.uniform(random_keys[0], (1, IMAGE_ROWS, IMAGE_COLUMNS), jnp.float32, math.log(low_end), math.log(high_end))
    column_weighting = jnp.exp(logs)
    surface_bumpiness = jax.random.uniform(random_keys[1], (VIEW_CELLS, IMAGE_ROWS, IMAGE_COLUMNS), jnp.float32, 0.5, 1.5)
    spike_row_indices = jax.random.randint(random_keys[2], (3,), 0, VIEW_CELLS)
    slice_depth_index = jnp.arange(VIEW_CELLS)
    spike_active = jnp.any(slice_depth_index[:, None] == spike_row_indices[None, :], axis=1).astype(jnp.float32)
    spike_multiplier = jax.random.uniform(random_keys[3], (1, IMAGE_ROWS, IMAGE_COLUMNS), jnp.float32, 0.5, 1.5)
    solute_field_value = column_weighting * surface_bumpiness + 0.7 * spike_active[:, None, None] * spike_multiplier
    return solute_field_value.astype(jnp.bfloat16)


def draw_depth_rank(key, part):
    brick_count = VIEW_CELLS // CZ
    flipped = jax.random.randint(key, (), 0, 2)
    positions = jnp.arange(brick_count)
    return jnp.where(flipped == 1, brick_count - 1 - positions, positions).astype(jnp.int32)


def draw_piece_home(key, part):
    tile_count = IMAGE_ROWS // BY
    random_keys = jax.random.split(key, 4)
    doubles = jax.random.randint(random_keys[0], (), 1, tile_count // 2 + 1)
    shuffle = jax.random.permutation(random_keys[1], tile_count)
    counts = jnp.where(shuffle < doubles, 2, jnp.where(shuffle < 2 * doubles, 0, 1)).astype(jnp.int32)
    bounds = jnp.cumsum(counts)
    permuter = jax.vmap(partial(jax.random.permutation, x=PPD))
    ranks = permuter(jax.random.split(random_keys[2], tile_count)).astype(jnp.int32)
    offsets = jnp.sum((bounds[None, None, :] <= ranks[:, :, None]).astype(jnp.int32), axis=2)
    owners = (jnp.arange(tile_count, dtype=jnp.int32)[:, None] + offsets) % tile_count
    slots = permuter(jax.random.split(random_keys[3], tile_count)).astype(jnp.int32)
    homes = owners * PPD + slots[owners, ranks]
    return homes.reshape(-1).astype(jnp.int32)


def setup_inputs(seed: int = 0) -> dict:
    arg_keys = jax.random.split(jax.random.key(seed), 4)
    density = draw_density(jax.random.fold_in(arg_keys[3], 71), 0)
    depth_rank = draw_depth_rank(jax.random.fold_in(arg_keys[3], 71), 0)
    piece_home = draw_piece_home(jax.random.fold_in(arg_keys[3], 71), 0)
    return {"density": density, "depth_rank": depth_rank, "piece_home": piece_home}


EXTINCT = 0.5
LIGHT_Z = 0.6
LIGHT_Y = 0.48
LIGHT_X = 0.64
SHARPNESS = 6.0
BACKDROP = (0.08, 0.1, 0.14)


def lighting(padded):
    center = padded[1:-1, 1:-1, :]
    grad_z = 0.5 * (padded[2:, 1:-1, :] - padded[:-2, 1:-1, :])
    grad_y = 0.5 * (padded[1:-1, 2:, :] - padded[1:-1, :-2, :])
    padded_x = jnp.pad(center, ((0, 0), (0, 0), (1, 1)))
    grad_x = 0.5 * (padded_x[:, :, 2:] - padded_x[:, :, :-2])
    facing = LIGHT_Z * grad_z + LIGHT_Y * grad_y + LIGHT_X * grad_x
    shading = 0.35 + 0.65 * (0.5 + 0.5 * jnp.tanh(SHARPNESS * facing))
    return center, shading


def emission(center):
    logged = jnp.log(center + 0.01)
    return (jax.nn.sigmoid(logged + 3.0), 0.5 + 0.5 * jnp.cos(1.7 * logged), jax.nn.sigmoid(-(logged + 2.5)))


def reference(density, depth_rank, piece_home):
    ascend = depth_rank[0] == 0
    padded = jnp.pad(density, ((1, 1), (1, 1), (0, 0)))
    backdrop = jnp.array(BACKDROP, jnp.float32)[:, None, None]

    def one_block(block_index):
        first_row = (block_index * BY).astype(jnp.int32)
        window = lax.dynamic_slice_in_dim(padded, first_row, BY + 2, 1).astype(jnp.float32)
        center, shading = lighting(window)
        optical = EXTINCT * center
        forward = lax.cumsum(optical, 0) - optical
        backward = lax.cumsum(optical, 0, reverse=True) - optical
        before = jnp.where(ascend, forward, backward)
        weight = jnp.exp(-before) * (-jnp.expm1(-optical)) * shading
        colors = emission(center)
        radiance = jnp.stack([jnp.sum(weight * channel, axis=0) for channel in colors])
        through = jnp.exp(-jnp.sum(optical, axis=0))
        return radiance + through[None] * backdrop

    finals = lax.map(one_block, jnp.arange(N_TILE, dtype=jnp.int32))
    pieces = finals.reshape(N_TILE, 3, N_DEPTH, PPD, PR)
    pieces = pieces.transpose(1, 2, 0, 3, 4).reshape(3, N_DEPTH, PIECES, PR)
    display = jnp.zeros_like(pieces).at[:, :, piece_home, :].set(pieces)
    return display
```

```python
import math
import jax
import jax.numpy as jnp
import numpy as np
from jax import lax
from jax.experimental import pallas as pl
from jax.experimental.pallas import tpu as pltpu
from jax.sharding import PartitionSpec as P

MOST = 2
NONE = -1

EXTINCT = 0.5
LIGHT_Z = 0.6
LIGHT_Y = 0.48
LIGHT_X = 0.64
SHARPNESS = 6.0
BACKDROP = (0.08, 0.1, 0.14)

PAD = 128
CB = 256
MC = 128
EDGE = 8
SIG_A = math.exp(-3.0)
SIG_B = math.exp(-2.5)
SHIFT = math.pi / 2 / (0.85 * math.log(2))
LEAD = 6.138231308051623e-10
SINSQ = (141379137.46788317, -4089655.3240788155, 47304.237438791075, -291.0939487912164)
UNIT = 65535.0
LOW = 65535


def stencils(rows):
    wy, wz = LIGHT_Y / LIGHT_X, LIGHT_Z / LIGHT_X
    left = np.zeros((rows, 3 * rows + 2 * EDGE), np.float32)
    for r in range(rows):
        left[r, r] = -wz
        left[r, 2 * rows + 2 * EDGE + r] = wz
        if r < rows - 1:
            left[r, rows + r + 1] = wy
        if r > 0:
            left[r, rows + r - 1] = -wy
    left[0, 2 * rows + EDGE - 1] = -wy
    left[rows - 1, 2 * rows + EDGE] = wy
    right = np.zeros((CB + 2 * PAD, CB), np.float32)
    for c in range(CB):
        right[c + PAD + 1, c] = 1.0
        right[c + PAD - 1, c] = -1.0
    return jnp.asarray(left, jnp.bfloat16), jnp.asarray(right, jnp.bfloat16)


def make_facing(d, g_pair, dens_pair, left, right, rows, zc):
    def facing(block, slot, chunk):
        z0 = chunk * zc
        g, dens16 = g_pair[slot], dens_pair[slot]
        c0 = pl.multiple_of(block * CB, CB)
        c1 = pl.multiple_of(block * CB + PAD, PAD)
        wide = d[pl.ds(z0 + 1, zc), 0:rows, pl.ds(c0, CB + 2 * PAD)]
        dx = jnp.dot(wide.reshape(zc * rows, CB + 2 * PAD), right[...],
                     preferred_element_type=jnp.float32)
        dens16[pl.ds(z0, zc)] = wide[:, :, PAD:PAD + CB]
        for i in range(zc):
            tall = jnp.concatenate([
                d[z0 + i, 0:rows, pl.ds(c1, CB)],
                d[z0 + i + 1, :, pl.ds(c1, CB)],
                d[z0 + i + 2, 0:rows, pl.ds(c1, CB)]], axis=0)
            dyz = jnp.dot(left[...], tall, preferred_element_type=jnp.float32)
            g[z0 + i] = dyz + dx[i * rows:(i + 1) * rows]

    return facing


def march(dens16, g, ascend, r0, lanes, band_rows, cells):
    bias = (0.35 + 0.65 * 0.5) / (0.65 * 0.5)
    zero = jnp.zeros((band_rows, MC), jnp.float32)
    trans = zero + 1.0
    total = m0 = m1 = wave = zero
    for k in range(cells):
        z = jnp.where(ascend, k, cells - 1 - k)
        dens = dens16[z, pl.ds(r0, band_rows), lanes].astype(jnp.float32)
        face = g[z, pl.ds(r0, band_rows), lanes]
        shade = jnp.tanh(face * (0.5 * SHARPNESS * LIGHT_X)) + bias
        after = trans * jnp.exp2(dens * (-EXTINCT * math.log2(math.e)))
        ws = (trans - after) * shade
        trans = after
        v = jnp.log2(dens + 0.01) + SHIFT
        q = v * v
        c = q + SINSQ[-1]
        for coef in SINSQ[-2::-1]:
            c = c * q + coef
        c = c * q
        total = total + ws
        m0 = m0 + ws * (1.0 / (dens + (0.01 + SIG_A)))
        m1 = m1 + ws * (1.0 / (dens + (0.01 + SIG_B)))
        wave = wave + ws * (c * (1.0 / LEAD - c))
    scale = 0.65 * 0.5
    return (
        scale * (total - SIG_A * m0),
        (scale * 4 * LEAD * LEAD) * wave,
        (scale * SIG_B) * m1,
        trans,
    )


def coded(value):
    return jnp.clip(value + 0.5, 0.0, UNIT).astype(jnp.int32)


def join(low, high):
    return low | (high << 16)


def low_part(word):
    return (word & LOW).astype(jnp.float32)


def high_part(word):
    return lax.shift_right_logical(word, 16).astype(jnp.float32)


def brick_kernel(nd, nt, ppd, rank, home, dens, names, left, right, inbox, arrived,
                 d, g0, g1, dens0, dens1, out, recv, fin, outbox, route,
                 dens_sem, hsend, hrecv, dsend, drecv, tsend, trecv, lsend, lrecv):
    cells, rows, cols = dens.shape
    nb, parts = cols // CB, CB // MC
    its = nd * parts
    zc = cells // its
    qrows = rows // nd
    width, rpp = outbox.shape[3], outbox.shape[2]
    groups = tsend.shape[0]
    me_d, me_t = lax.axis_index("depth"), lax.axis_index("tile")
    mesh_ids = pl.DeviceIdType.MESH

    barrier = pltpu.get_barrier_semaphore()

    @pl.loop(1, nt)
    def _(o):
        pl.semaphore_signal(barrier, inc=1, device_id=(me_d, lax.rem(me_t + o, nt)), device_id_type=mesh_ids)

    for k in range(1, nd):
        pl.semaphore_signal(barrier, inc=1, device_id=(lax.rem(me_d + k, nd), me_t), device_id_type=mesh_ids)

    def cols_of(b):
        return pl.ds(pl.multiple_of(b * CB, CB), CB)

    def pads_of(b):
        return pl.ds(pl.multiple_of(b * CB + PAD, PAD), CB)

    def dens_copy(b):
        return pltpu.make_async_copy(
            dens.at[:, :, cols_of(b)], d.at[pl.ds(1, cells), pl.ds(0, rows), pads_of(b)], dens_sem.at[b])

    def halo(kind, b):
        inner = pl.ds(1, cells)
        src, dst, step = (
            (dens.at[cells - 1, :, cols_of(b)], d.at[0, pl.ds(0, rows), pads_of(b)], 1),
            (dens.at[0, :, cols_of(b)], d.at[cells + 1, pl.ds(0, rows), pads_of(b)], nd - 1),
            (dens.at[:, pl.ds(rows - EDGE, EDGE), cols_of(b)],
             d.at[inner, pl.ds(rows, EDGE), pads_of(b)], 1),
            (dens.at[:, pl.ds(0, EDGE), cols_of(b)],
             d.at[inner, pl.ds(rows + EDGE, EDGE), pads_of(b)], nt - 1),
        )[kind]
        to = (lax.rem(me_d + step, nd), me_t) if kind < 2 else (me_d, lax.rem(me_t + step, nt))
        return pltpu.make_async_remote_copy(
            src_ref=src, dst_ref=dst, send_sem=hsend.at[kind, b], recv_sem=hrecv.at[kind, b],
            device_id=to, device_id_type=mesh_ids)

    sends = (me_d < nd - 1, me_d > 0, me_t < nt - 1, me_t > 0)
    gets = (me_d > 0, me_d < nd - 1, me_t > 0, me_t < nt - 1)

    @pl.loop(0, nb)
    def _(b):
        dens_copy(b).start()

    side = jnp.zeros((cells + 2, rows + 2 * EDGE, PAD), d.dtype)
    d[:, :, :PAD] = side
    d[:, :, cols + PAD:] = side

    @pl.when(me_d == 0)
    def _():
        d[0, 0:rows, PAD:cols + PAD] = jnp.zeros((rows, cols), d.dtype)

    @pl.when(me_d == nd - 1)
    def _():
        d[cells + 1, 0:rows, PAD:cols + PAD] = jnp.zeros((rows, cols), d.dtype)

    edge = jnp.zeros((cells, EDGE, cols), d.dtype)

    @pl.when(me_t == 0)
    def _():
        d[1:cells + 1, rows:rows + EDGE, PAD:cols + PAD] = edge

    @pl.when(me_t == nt - 1)
    def _():
        d[1:cells + 1, rows + EDGE:, PAD:cols + PAD] = edge

    pl.semaphore_wait(barrier, nt - 1 + nd - 1)

    @pl.loop(0, nb)
    def _(b):
        for kind in range(4):
            @pl.when(sends[kind])
            def _():
                halo(kind, b).start()

    def label_copy(o):
        return pltpu.make_async_remote_copy(
            src_ref=names, dst_ref=arrived.at[o], send_sem=lsend.at[o], recv_sem=lrecv.at[o],
            device_id=(me_d, lax.rem(me_t + o, nt)), device_id_type=mesh_ids)

    own_labels = pltpu.make_async_copy(names, arrived.at[0], lsend.at[0])
    own_labels.start()

    @pl.loop(1, nt)
    def _(o):
        label_copy(o).start()

    @pl.loop(0, nt)
    def _(o):
        start = lax.rem(me_t + o, nt) * ppd
        first, last = ppd - 1, 0
        for p in range(ppd):
            h = home[p] - start
            hit = (h >= 0) & (h < ppd)
            first = jnp.where(hit, jnp.minimum(first, p), first)
            last = jnp.where(hit, p, last)
        route[o, 0] = first
        route[o, 1] = last

    def arrive(b):
        dens_copy(b).wait()
        for kind in range(4):
            @pl.when(gets[kind])
            def _():
                halo(kind, b).wait_recv()

    ascend = rank[0] == 0
    g_pair, dens_pair = (g0, g1), (dens0, dens1)
    facing = make_facing(d, g_pair, dens_pair, left, right, rows, zc)

    def depth_copy(k, b, src):
        to = lax.rem(me_d + k, nd)
        return pltpu.make_async_remote_copy(
            src_ref=out.at[:, pl.ds(pl.multiple_of(to * qrows, 8), qrows), cols_of(b)],
            dst_ref=recv.at[src, :, :, cols_of(b)],
            send_sem=dsend.at[b, k], recv_sem=drecv.at[b, src],
            device_id=(to, me_t), device_id_type=mesh_ids)

    def keep_own(b):
        mine = out[:, pl.ds(pl.multiple_of(me_d * qrows, 8), qrows), cols_of(b)]
        recv[me_d, :, :, cols_of(b)] = mine

    def brick(i, b):
        one, two = recv[i, 0, :, cols_of(b)], recv[i, 1, :, cols_of(b)]
        colors = jnp.stack([low_part(one), high_part(one), low_part(two)])
        return colors, high_part(two) * (1.0 / UNIT)

    def composite(b):
        for k in range(1, nd):
            depth_copy(k, b, lax.rem(me_d + k, nd)).wait_recv()
        color, trans = brick(0, b)
        for i in range(1, nd):
            new, new_trans = brick(i, b)
            front, back = jnp.where(ascend, color, new), jnp.where(ascend, new, color)
            color = front + jnp.where(ascend, trans, new_trans)[None] * back
            trans = trans * new_trans
        for ch in range(3):
            fin[ch, :, cols_of(b)] = coded(color[ch] + trans * (BACKDROP[ch] * UNIT))

    def tile_copy(o, part, window):
        return pltpu.make_async_remote_copy(
            src_ref=outbox.at[o, :, :, window], dst_ref=inbox.at[o, :, :, window],
            send_sem=tsend.at[part, o], recv_sem=trecv.at[part, o],
            device_id=(me_d, lax.rem(me_t + o, nt)), device_id_type=mesh_ids)

    def tile_own(part, window):
        return pltpu.make_async_copy(
            outbox.at[0, :, :, window], inbox.at[0, :, :, window], tsend.at[part, 0])

    def ship(part, window):
        def piece(p, r):
            if width == cols:
                return fin[:, pl.ds(p * rpp + r, 1), window]
            per = cols // width
            c = pl.multiple_of(lax.rem(p, per) * width, width)
            return fin[:, pl.ds(lax.div(p, per), 1), pl.ds(c, width)]

        @pl.loop(0, nt)
        def _(o):
            for r in range(rpp):
                outbox[o, :, r:r + 1, window] = join(piece(route[o, 0], r), piece(route[o, 1], r))

        tile_own(part, window).start()

        @pl.loop(1, nt)
        def _(o):
            tile_copy(o, part, window).start()

    arrive(0)
    arrive(1)

    @pl.loop(0, its)
    def _(it):
        facing(0, 0, it)

    def finish(b):
        composite(b)
        if groups == nb:
            ship(b, cols_of(b))

    def step(b, slot):
        @pl.when(b + 2 < nb)
        def _():
            arrive(b + 2)

        ahead = lax.rem(b + 1, nb)

        @pl.loop(0, its)
        def _(it):
            facing(ahead, 1 - slot, it)
            k = lax.div(it, parts) + 1
            part = lax.rem(it, parts)
            band = pl.multiple_of(lax.rem(me_d + k, nd) * qrows, 8)
            vals = march(dens_pair[slot], g_pair[slot], ascend, band,
                         pl.ds(pl.multiple_of(part * MC, MC), MC), qrows, cells)
            c0, c1, c2, tr = (coded(val * UNIT) for val in vals)
            lanes = pl.ds(pl.multiple_of(b * CB + part * MC, MC), MC)
            out[0, pl.ds(band, qrows), lanes] = join(c0, c1)
            out[1, pl.ds(band, qrows), lanes] = join(c2, tr)

            @pl.when((part == parts - 1) & (k < nd))
            def _():
                depth_copy(k, b, me_d).start()

        keep_own(b)

        @pl.when(b > 0)
        def _():
            finish(b - 1)

    @pl.loop(0, nb // 2)
    def _(pair):
        step(2 * pair, 0)
        step(2 * pair + 1, 1)

    finish(nb - 1)
    if groups != nb:
        ship(0, pl.ds(0, width))

    own_labels.wait()

    @pl.loop(1, nt)
    def _(o):
        label_copy(o).wait()

    @pl.loop(0, groups)
    def _(part):
        window = cols_of(part) if groups == nb else pl.ds(0, width)
        tile_own(part, window).wait()

        @pl.loop(1, nt)
        def _(o):
            tile_copy(o, part, window).wait()

    @pl.loop(0, nb)
    def _(b):
        for k in range(1, nd):
            depth_copy(k, b, me_d).wait_send()

    for kind in range(4):
        @pl.when(sends[kind])
        def _():
            @pl.loop(0, nb)
            def _(b):
                halo(kind, b).wait_send()


def place_kernel(arrived, inbox, display):
    nt, rpp, width = inbox.shape[0], inbox.shape[2], inbox.shape[3]
    ppd = display.shape[2]
    start = lax.axis_index("tile") * ppd

    @pl.loop(0, nt)
    def _(o):
        first, last = jnp.int32(NONE), jnp.int32(NONE)
        for p in range(ppd):
            h = arrived[o, 0, p] - start
            hit = (h >= 0) & (h < ppd)
            first = jnp.where(hit & (first == NONE), h, first)
            last = jnp.where(hit, h, last)

        def put(label, part):
            for r in range(rpp):
                piece = part(inbox[o, :, r:r + 1, :]) * (1.0 / UNIT)
                display[:, 0, pl.ds(label, 1), r * width:(r + 1) * width] = piece

        @pl.when(first != NONE)
        def _():
            put(first, low_part)

        @pl.when(last != first)
        def _():
            put(last, high_part)


def on_device(density, depth_rank, piece_home):
    cells, rows, cols = density.shape
    nd, nt = lax.axis_size("depth"), lax.axis_size("tile")
    ppd = piece_home.shape[0]
    qrows = rows // nd
    piece_len = qrows * cols // ppd
    width = min(piece_len, cols)
    rpp = piece_len // width
    nb = cols // CB
    groups = nb if width == cols else 1

    names = piece_home.reshape(1, ppd)
    left, right = stencils(rows)
    anyspec = pl.BlockSpec(memory_space=pl.ANY)
    vmem = pl.BlockSpec(memory_space=pltpu.VMEM)
    smem = pl.BlockSpec(memory_space=pltpu.SMEM)
    dma = pltpu.SemaphoreType.DMA
    f32, i32 = jnp.float32, jnp.int32
    inbox, arrived = pl.pallas_call(
        lambda *refs: brick_kernel(nd, nt, ppd, *refs),
        out_shape=(jax.ShapeDtypeStruct((nt, 3, rpp, width), i32),
                   jax.ShapeDtypeStruct((nt, 1, ppd), i32)),
        in_specs=[smem, smem] + [anyspec] * 2 + [vmem] * 2,
        out_specs=(anyspec, anyspec),
        scratch_shapes=[
            pltpu.VMEM((cells + 2, rows + 2 * EDGE, cols + 2 * PAD), jnp.bfloat16),
            pltpu.VMEM((cells, rows, CB), f32),
            pltpu.VMEM((cells, rows, CB), f32),
            pltpu.VMEM((cells, rows, CB), jnp.bfloat16),
            pltpu.VMEM((cells, rows, CB), jnp.bfloat16),
            pltpu.VMEM((2, rows, cols), i32),
            pltpu.VMEM((nd, 2, qrows, cols), i32),
            pltpu.VMEM((3, qrows, cols), i32),
            pltpu.VMEM((nt, 3, rpp, width), i32),
            pltpu.SMEM((nt, MOST), i32),
            dma((nb,)), dma((4, nb)), dma((4, nb)), dma((nb, nd)), dma((nb, nd)),
            dma((groups, nt)), dma((groups, nt)), dma((nt,)), dma((nt,)),
        ],
        compiler_params=pltpu.CompilerParams(
            collective_id=0, has_side_effects=True, vmem_limit_bytes=56 * 1024 * 1024),
    )(depth_rank, piece_home, density, names, left, right)
    return pl.pallas_call(
        place_kernel,
        out_shape=jax.ShapeDtypeStruct((3, 1, ppd, piece_len), f32),
        in_specs=[smem, vmem],
        out_specs=vmem,
    )(arrived, inbox)


def solution(mesh):
    in_specs = (P("depth", "tile", None), P(), P("tile"))
    out_specs = P(None, "depth", "tile", None)
    return jax.shard_map(
        on_device, mesh=mesh, in_specs=in_specs, out_specs=out_specs, check_vma=False
    )
```

```python
import math
import jax
import jax.numpy as jnp
import numpy as np
from jax import lax
from jax.experimental import pallas as pl
from jax.experimental.pallas import tpu as pltpu
from jax.sharding import PartitionSpec as P

MOST = 2
NONE = -1

EXTINCT = 0.5
LIGHT_Z = 0.6
LIGHT_Y = 0.48
LIGHT_X = 0.64
SHARPNESS = 6.0
BACKDROP = (0.08, 0.1, 0.14)

PAD = 128
CB = 256
MC = 128
EDGE = 8
SIG_A = math.exp(-3.0)
SIG_B = math.exp(-2.5)
SHIFT = math.pi / 2 / (0.85 * math.log(2))
LEAD = 6.138231308051623e-10
SINSQ = (141379137.46788317, -4089655.3240788155, 47304.237438791075, -291.0939487912164)
UNIT = 65535.0
LOW = 65535


def stencils(rows):
    wy, wz = LIGHT_Y / LIGHT_X, LIGHT_Z / LIGHT_X
    left = np.zeros((rows, 3 * rows + 2 * EDGE), np.float32)
    for r in range(rows):
        left[r, r] = -wz
        left[r, 2 * rows + 2 * EDGE + r] = wz
        if r < rows - 1:
            left[r, rows + r + 1] = wy
        if r > 0:
            left[r, rows + r - 1] = -wy
    left[0, 2 * rows + EDGE - 1] = -wy
    left[rows - 1, 2 * rows + EDGE] = wy
    right = np.zeros((CB + 2 * PAD, CB), np.float32)
    for c in range(CB):
        right[c + PAD + 1, c] = 1.0
        right[c + PAD - 1, c] = -1.0
    return jnp.asarray(left, jnp.bfloat16), jnp.asarray(right, jnp.bfloat16)


def make_facing(d, g, dens16, left, right, rows):
    def begin(block, slot, z):
        c0 = pl.multiple_of(block * CB, CB)
        c1 = pl.multiple_of(block * CB + PAD, PAD)
        wide = d[z + 1, 0:rows, pl.ds(c0, CB + 2 * PAD)]
        tall = jnp.concatenate([
            d[z, 0:rows, pl.ds(c1, CB)],
            d[z + 1, :, pl.ds(c1, CB)],
            d[z + 2, 0:rows, pl.ds(c1, CB)]], axis=0)
        dx = jnp.dot(wide, right[...], preferred_element_type=jnp.float32)
        both = dx + jnp.dot(left[...], tall, preferred_element_type=jnp.float32)
        dens16[slot, z] = wide[:, PAD:PAD + CB]
        return slot, z, both

    def end(slot, z, both):
        g[slot, z] = both

    return begin, end


def march(dens16, g, slot, ascend, r0, lanes, band_rows, cells, zc, begin, end):
    bias = (0.35 + 0.65 * 0.5) / (0.65 * 0.5)
    zero = jnp.zeros((band_rows, MC), jnp.float32)
    trans = zero + 1.0
    total = m0 = m1 = wave = zero
    for k in range(cells):
        if k == 0:
            held = begin(0)
        turn = (k * 16 - 6 * cells) // (3 * cells)
        if k * 16 == (6 + 3 * turn) * cells and 0 <= turn < zc:
            end(*held)
            if turn + 1 < zc:
                held = begin(turn + 1)
        z = jnp.where(ascend, k, cells - 1 - k)
        dens = dens16[slot, z, pl.ds(r0, band_rows), lanes].astype(jnp.float32)
        face = g[slot, z, pl.ds(r0, band_rows), lanes]
        shade = jnp.tanh(face * (0.5 * SHARPNESS * LIGHT_X)) + bias
        after = trans * jnp.exp2(dens * (-EXTINCT * math.log2(math.e)))
        ws = (trans - after) * shade
        trans = after
        v = jnp.log2(dens + 0.01) + SHIFT
        q = v * v
        c = q + SINSQ[-1]
        for coef in SINSQ[-2::-1]:
            c = c * q + coef
        c = c * q
        total = total + ws
        m0 = m0 + ws * (1.0 / (dens + (0.01 + SIG_A)))
        m1 = m1 + ws * (1.0 / (dens + (0.01 + SIG_B)))
        wave = wave + ws * (c * (1.0 / LEAD - c))
    scale = 0.65 * 0.5
    return (
        scale * (total - SIG_A * m0),
        (scale * 4 * LEAD * LEAD) * wave,
        (scale * SIG_B) * m1,
        trans,
    )


def coded(value):
    return jnp.clip(value + 0.5, 0.0, UNIT).astype(jnp.int32)


def join(low, high):
    return low | (high << 16)


def low_part(word):
    return (word & LOW).astype(jnp.float32)


def high_part(word):
    return lax.shift_right_logical(word, 16).astype(jnp.float32)


def brick_kernel(nd, nt, ppd, rank, home, dens, names, left, right, inbox, arrived,
                 d, g, dens16, out, recv, fin, outbox, route,
                 dens_sem, hsend, hrecv, dsend, drecv, tsend, trecv, lsend, lrecv):
    cells, rows, cols = dens.shape
    nb, parts = cols // CB, CB // MC
    its = nd * parts
    zc = cells // its
    qrows = rows // nd
    width, rpp = outbox.shape[3], outbox.shape[2]
    groups = tsend.shape[0]
    me_d, me_t = lax.axis_index("depth"), lax.axis_index("tile")
    mesh_ids = pl.DeviceIdType.MESH

    barrier = pltpu.get_barrier_semaphore()

    @pl.loop(1, nt)
    def _(o):
        pl.semaphore_signal(barrier, inc=1, device_id=(me_d, lax.rem(me_t + o, nt)), device_id_type=mesh_ids)

    for k in range(1, nd):
        pl.semaphore_signal(barrier, inc=1, device_id=(lax.rem(me_d + k, nd), me_t), device_id_type=mesh_ids)

    def cols_of(b):
        return pl.ds(pl.multiple_of(b * CB, CB), CB)

    def pads_of(b):
        return pl.ds(pl.multiple_of(b * CB + PAD, PAD), CB)

    def dens_copy(b):
        return pltpu.make_async_copy(
            dens.at[:, :, cols_of(b)], d.at[pl.ds(1, cells), pl.ds(0, rows), pads_of(b)], dens_sem.at[b])

    def halo(kind, b):
        inner = pl.ds(1, cells)
        src, dst, step = (
            (dens.at[cells - 1, :, cols_of(b)], d.at[0, pl.ds(0, rows), pads_of(b)], 1),
            (dens.at[0, :, cols_of(b)], d.at[cells + 1, pl.ds(0, rows), pads_of(b)], nd - 1),
            (dens.at[:, pl.ds(rows - EDGE, EDGE), cols_of(b)],
             d.at[inner, pl.ds(rows, EDGE), pads_of(b)], 1),
            (dens.at[:, pl.ds(0, EDGE), cols_of(b)],
             d.at[inner, pl.ds(rows + EDGE, EDGE), pads_of(b)], nt - 1),
        )[kind]
        to = (lax.rem(me_d + step, nd), me_t) if kind < 2 else (me_d, lax.rem(me_t + step, nt))
        return pltpu.make_async_remote_copy(
            src_ref=src, dst_ref=dst, send_sem=hsend.at[kind, b], recv_sem=hrecv.at[kind, b],
            device_id=to, device_id_type=mesh_ids)

    sends = (me_d < nd - 1, me_d > 0, me_t < nt - 1, me_t > 0)
    gets = (me_d > 0, me_d < nd - 1, me_t > 0, me_t < nt - 1)

    @pl.loop(0, nb)
    def _(b):
        dens_copy(b).start()

    side = jnp.zeros((cells + 2, rows + 2 * EDGE, PAD), d.dtype)
    d[:, :, :PAD] = side
    d[:, :, cols + PAD:] = side

    @pl.when(me_d == 0)
    def _():
        d[0, 0:rows, PAD:cols + PAD] = jnp.zeros((rows, cols), d.dtype)

    @pl.when(me_d == nd - 1)
    def _():
        d[cells + 1, 0:rows, PAD:cols + PAD] = jnp.zeros((rows, cols), d.dtype)

    edge = jnp.zeros((cells, EDGE, cols), d.dtype)

    @pl.when(me_t == 0)
    def _():
        d[1:cells + 1, rows:rows + EDGE, PAD:cols + PAD] = edge

    @pl.when(me_t == nt - 1)
    def _():
        d[1:cells + 1, rows + EDGE:, PAD:cols + PAD] = edge

    pl.semaphore_wait(barrier, nt - 1 + nd - 1)

    @pl.loop(0, nb)
    def _(b):
        for kind in range(4):
            @pl.when(sends[kind])
            def _():
                halo(kind, b).start()

    def label_copy(o):
        return pltpu.make_async_remote_copy(
            src_ref=names, dst_ref=arrived.at[o], send_sem=lsend.at[o], recv_sem=lrecv.at[o],
            device_id=(me_d, lax.rem(me_t + o, nt)), device_id_type=mesh_ids)

    own_labels = pltpu.make_async_copy(names, arrived.at[0], lsend.at[0])
    own_labels.start()

    @pl.loop(1, nt)
    def _(o):
        label_copy(o).start()

    @pl.loop(0, nt)
    def _(o):
        start = lax.rem(me_t + o, nt) * ppd
        first, last = ppd - 1, 0
        for p in range(ppd):
            h = home[p] - start
            hit = (h >= 0) & (h < ppd)
            first = jnp.where(hit, jnp.minimum(first, p), first)
            last = jnp.where(hit, p, last)
        route[o, 0] = first
        route[o, 1] = last

    def arrive(b):
        dens_copy(b).wait()
        for kind in range(4):
            @pl.when(gets[kind])
            def _():
                halo(kind, b).wait_recv()

    ascend = rank[0] == 0
    begin, end = make_facing(d, g, dens16, left, right, rows)

    def depth_copy(k, b, src):
        to = lax.rem(me_d + k, nd)
        return pltpu.make_async_remote_copy(
            src_ref=out.at[:, pl.ds(pl.multiple_of(to * qrows, 8), qrows), cols_of(b)],
            dst_ref=recv.at[src, :, :, cols_of(b)],
            send_sem=dsend.at[b, k], recv_sem=drecv.at[b, src],
            device_id=(to, me_t), device_id_type=mesh_ids)

    def keep_own(b):
        mine = out[:, pl.ds(pl.multiple_of(me_d * qrows, 8), qrows), cols_of(b)]
        recv[me_d, :, :, cols_of(b)] = mine

    def brick(i, b):
        one, two = recv[i, 0, :, cols_of(b)], recv[i, 1, :, cols_of(b)]
        colors = jnp.stack([low_part(one), high_part(one), low_part(two)])
        return colors, high_part(two) * (1.0 / UNIT)

    def composite(b):
        for k in range(1, nd):
            depth_copy(k, b, lax.rem(me_d + k, nd)).wait_recv()
        color, trans = brick(0, b)
        for i in range(1, nd):
            new, new_trans = brick(i, b)
            front, back = jnp.where(ascend, color, new), jnp.where(ascend, new, color)
            color = front + jnp.where(ascend, trans, new_trans)[None] * back
            trans = trans * new_trans
        for ch in range(3):
            fin[ch, :, cols_of(b)] = coded(color[ch] + trans * (BACKDROP[ch] * UNIT))

    def tile_copy(o, part, window):
        return pltpu.make_async_remote_copy(
            src_ref=outbox.at[o, :, :, window], dst_ref=inbox.at[o, :, :, window],
            send_sem=tsend.at[part, o], recv_sem=trecv.at[part, o],
            device_id=(me_d, lax.rem(me_t + o, nt)), device_id_type=mesh_ids)

    def tile_own(part, window):
        return pltpu.make_async_copy(
            outbox.at[0, :, :, window], inbox.at[0, :, :, window], tsend.at[part, 0])

    def ship(part, window):
        def piece(p, r):
            if width == cols:
                return fin[:, pl.ds(p * rpp + r, 1), window]
            per = cols // width
            c = pl.multiple_of(lax.rem(p, per) * width, width)
            return fin[:, pl.ds(lax.div(p, per), 1), pl.ds(c, width)]

        @pl.loop(0, nt)
        def _(o):
            for r in range(rpp):
                outbox[o, :, r:r + 1, window] = join(piece(route[o, 0], r), piece(route[o, 1], r))

        tile_own(part, window).start()

        @pl.loop(1, nt)
        def _(o):
            tile_copy(o, part, window).start()

    arrive(0)
    arrive(1)

    @pl.loop(0, its)
    def _(it):
        for i in range(zc):
            end(*begin(0, 0, it * zc + i))

    def finish(b):
        composite(b)
        if groups == nb:
            ship(b, cols_of(b))

    @pl.loop(0, nb)
    def _(b):
        slot = lax.rem(b, 2)

        @pl.when(b + 2 < nb)
        def _():
            arrive(b + 2)

        ahead = lax.rem(b + 1, nb)

        @pl.loop(0, its)
        def _(it):
            k = lax.div(it, parts) + 1
            part = lax.rem(it, parts)
            band = pl.multiple_of(lax.rem(me_d + k, nd) * qrows, 8)
            vals = march(dens16, g, slot, ascend, band,
                         pl.ds(pl.multiple_of(part * MC, MC), MC), qrows, cells, zc,
                         lambda i: begin(ahead, 1 - slot, it * zc + i), end)
            c0, c1, c2, tr = (coded(val * UNIT) for val in vals)
            lanes = pl.ds(pl.multiple_of(b * CB + part * MC, MC), MC)
            out[0, pl.ds(band, qrows), lanes] = join(c0, c1)
            out[1, pl.ds(band, qrows), lanes] = join(c2, tr)

            @pl.when((part == parts - 1) & (k < nd))
            def _():
                depth_copy(k, b, me_d).start()

        keep_own(b)

        @pl.when(b > 0)
        def _():
            finish(b - 1)

    finish(nb - 1)
    if groups != nb:
        ship(0, pl.ds(0, width))

    own_labels.wait()

    @pl.loop(1, nt)
    def _(o):
        label_copy(o).wait()

    @pl.loop(0, groups)
    def _(part):
        window = cols_of(part) if groups == nb else pl.ds(0, width)
        tile_own(part, window).wait()

        @pl.loop(1, nt)
        def _(o):
            tile_copy(o, part, window).wait()

    @pl.loop(0, nb)
    def _(b):
        for k in range(1, nd):
            depth_copy(k, b, me_d).wait_send()

    for kind in range(4):
        @pl.when(sends[kind])
        def _():
            @pl.loop(0, nb)
            def _(b):
                halo(kind, b).wait_send()


def place_kernel(arrived, inbox, display):
    nt, rpp, width = inbox.shape[0], inbox.shape[2], inbox.shape[3]
    ppd = display.shape[2]
    start = lax.axis_index("tile") * ppd

    @pl.loop(0, nt)
    def _(o):
        first, last = jnp.int32(NONE), jnp.int32(NONE)
        for p in range(ppd):
            h = arrived[o, 0, p] - start
            hit = (h >= 0) & (h < ppd)
            first = jnp.where(hit & (first == NONE), h, first)
            last = jnp.where(hit, h, last)

        def put(label, part):
            for r in range(rpp):
                piece = part(inbox[o, :, r:r + 1, :]) * (1.0 / UNIT)
                display[:, 0, pl.ds(label, 1), r * width:(r + 1) * width] = piece

        @pl.when(first != NONE)
        def _():
            put(first, low_part)

        @pl.when(last != first)
        def _():
            put(last, high_part)


def on_device(density, depth_rank, piece_home):
    cells, rows, cols = density.shape
    nd, nt = lax.axis_size("depth"), lax.axis_size("tile")
    ppd = piece_home.shape[0]
    qrows = rows // nd
    piece_len = qrows * cols // ppd
    width = min(piece_len, cols)
    rpp = piece_len // width
    nb = cols // CB
    groups = nb if width == cols else 1

    names = piece_home.reshape(1, ppd)
    left, right = stencils(rows)
    anyspec = pl.BlockSpec(memory_space=pl.ANY)
    vmem = pl.BlockSpec(memory_space=pltpu.VMEM)
    smem = pl.BlockSpec(memory_space=pltpu.SMEM)
    dma = pltpu.SemaphoreType.DMA
    f32, i32 = jnp.float32, jnp.int32
    inbox, arrived = pl.pallas_call(
        lambda *refs: brick_kernel(nd, nt, ppd, *refs),
        out_shape=(jax.ShapeDtypeStruct((nt, 3, rpp, width), i32),
                   jax.ShapeDtypeStruct((nt, 1, ppd), i32)),
        in_specs=[smem, smem] + [anyspec] * 2 + [vmem] * 2,
        out_specs=(anyspec, anyspec),
        scratch_shapes=[
            pltpu.VMEM((cells + 2, rows + 2 * EDGE, cols + 2 * PAD), jnp.bfloat16),
            pltpu.VMEM((2, cells, rows, CB), f32),
            pltpu.VMEM((2, cells, rows, CB), jnp.bfloat16),
            pltpu.VMEM((2, rows, cols), i32),
            pltpu.VMEM((nd, 2, qrows, cols), i32),
            pltpu.VMEM((3, qrows, cols), i32),
            pltpu.VMEM((nt, 3, rpp, width), i32),
            pltpu.SMEM((nt, MOST), i32),
            dma((nb,)), dma((4, nb)), dma((4, nb)), dma((nb, nd)), dma((nb, nd)),
            dma((groups, nt)), dma((groups, nt)), dma((nt,)), dma((nt,)),
        ],
        compiler_params=pltpu.CompilerParams(
            collective_id=0, has_side_effects=True, vmem_limit_bytes=56 * 1024 * 1024),
    )(depth_rank, piece_home, density, names, left, right)
    return pl.pallas_call(
        place_kernel,
        out_shape=jax.ShapeDtypeStruct((3, 1, ppd, piece_len), f32),
        in_specs=[smem, vmem],
        out_specs=vmem,
    )(arrived, inbox)


def solution(mesh):
    in_specs = (P("depth", "tile", None), P(), P("tile"))
    out_specs = P(None, "depth", "tile", None)
    return jax.shard_map(
        on_device, mesh=mesh, in_specs=in_specs, out_specs=out_specs, check_vma=False
    )
```

```python
import math
import jax
import jax.numpy as jnp
import numpy as np
from jax import lax
from jax.experimental import pallas as pl
from jax.experimental.pallas import tpu as pltpu
from jax.sharding import PartitionSpec as P

MOST = 2
NONE = -1

EXTINCT = 0.5
LIGHT_Z = 0.6
LIGHT_Y = 0.48
LIGHT_X = 0.64
SHARPNESS = 6.0
BACKDROP = (0.08, 0.1, 0.14)

PAD = 128
CB = 256
MC = 128
EDGE = 8
SIG_A = math.exp(-3.0)
SIG_B = math.exp(-2.5)
SHIFT = math.pi / 2 / (0.85 * math.log(2))
LEAD = 6.138231308051623e-10
SINSQ = (141379137.46788317, -4089655.3240788155, 47304.237438791075, -291.0939487912164)
UNIT = 65535.0
LOW = 65535


def stencils(rows):
    wy, wz = LIGHT_Y / LIGHT_X, LIGHT_Z / LIGHT_X
    left = np.zeros((rows, 3 * rows + 2 * EDGE), np.float32)
    for r in range(rows):
        left[r, r] = -wz
        left[r, 2 * rows + 2 * EDGE + r] = wz
        if r < rows - 1:
            left[r, rows + r + 1] = wy
        if r > 0:
            left[r, rows + r - 1] = -wy
    left[0, 2 * rows + EDGE - 1] = -wy
    left[rows - 1, 2 * rows + EDGE] = wy
    right = np.zeros((CB + 2 * PAD, CB), np.float32)
    for c in range(CB):
        right[c + PAD + 1, c] = 1.0
        right[c + PAD - 1, c] = -1.0
    return jnp.asarray(left, jnp.bfloat16), jnp.asarray(right, jnp.bfloat16)


def make_facing(d, g, dens16, left, right, rows, zc):
    def across(block, chunk):
        wide = d[pl.ds(chunk * zc + 1, zc), 0:rows, pl.ds(pl.multiple_of(block * CB, CB), CB + 2 * PAD)]
        wide = wide.reshape(zc * rows, CB + 2 * PAD)
        return [jnp.dot(wide[:, h:h + CB], right[h:h + CB], preferred_element_type=jnp.float32)
                for h in range(0, CB + 2 * PAD, CB)]

    def begin(block, chunk, i):
        z = chunk * zc + i
        c1 = pl.multiple_of(block * CB + PAD, PAD)
        tall = jnp.concatenate([
            d[z, 0:rows, pl.ds(c1, CB)],
            d[z + 1, :, pl.ds(c1, CB)],
            d[z + 2, 0:rows, pl.ds(c1, CB)]], axis=0)
        return jnp.dot(left[...], tall, preferred_element_type=jnp.float32)

    def end(block, slot, chunk, i, dx, dyz):
        z = chunk * zc + i
        g[slot, z] = dyz + sum(part[i * rows:(i + 1) * rows] for part in dx)
        dens16[slot, z] = d[z + 1, 0:rows, pl.ds(pl.multiple_of(block * CB + PAD, PAD), CB)]

    return across, begin, end


def march(dens16, g, slot, ascend, r0, lanes, band_rows, cells, beside):
    bias = (0.35 + 0.65 * 0.5) / (0.65 * 0.5)
    zero = jnp.zeros((band_rows, MC), jnp.float32)
    trans = zero + 1.0
    total = m0 = m1 = wave = zero
    for k in range(cells):
        beside(k)
        z = jnp.where(ascend, k, cells - 1 - k)
        dens = dens16[slot, z, pl.ds(r0, band_rows), lanes].astype(jnp.float32)
        face = g[slot, z, pl.ds(r0, band_rows), lanes]
        shade = jnp.tanh(face * (0.5 * SHARPNESS * LIGHT_X)) + bias
        after = trans * jnp.exp2(dens * (-EXTINCT * math.log2(math.e)))
        ws = (trans - after) * shade
        trans = after
        v = jnp.log2(dens + 0.01) + SHIFT
        q = v * v
        c = q + SINSQ[-1]
        for coef in SINSQ[-2::-1]:
            c = c * q + coef
        c = c * q
        total = total + ws
        m0 = m0 + ws * (1.0 / (dens + (0.01 + SIG_A)))
        m1 = m1 + ws * (1.0 / (dens + (0.01 + SIG_B)))
        wave = wave + ws * (c * (1.0 / LEAD - c))
    scale = 0.65 * 0.5
    return (
        scale * (total - SIG_A * m0),
        (scale * 4 * LEAD * LEAD) * wave,
        (scale * SIG_B) * m1,
        trans,
    )


class Beside:
    def __init__(self, steps, planes, across, begin, end):
        self.across, self.begin, self.end = across, begin, end
        gap = steps // planes
        self.turns = {}
        for i in range(planes):
            self.turns.setdefault(i * gap, []).append((True, i))
            stop = min(i * gap + gap * 24 // 8, steps)
            self.turns.setdefault(stop, []).append((False, i))
        self.held, self.dx = {}, None

    def __call__(self, step):
        if step == 0:
            self.dx = self.across()
        for fresh, i in self.turns.get(step, ()):
            if fresh:
                self.held[i] = self.begin(i)
            else:
                self.end(i, self.dx, self.held[i])


def coded(value):
    return jnp.clip(value + 0.5, 0.0, UNIT).astype(jnp.int32)


def join(low, high):
    return low | (high << 16)


def low_part(word):
    return (word & LOW).astype(jnp.float32)


def high_part(word):
    return lax.shift_right_logical(word, 16).astype(jnp.float32)


def brick_kernel(nd, nt, ppd, rank, home, dens, names, left, right, inbox, arrived,
                 d, g, dens16, out, recv, fin, outbox, route,
                 dens_sem, hsend, hrecv, dsend, drecv, tsend, trecv, lsend, lrecv):
    cells, rows, cols = dens.shape
    nb, parts = cols // CB, CB // MC
    zc = cells // nd
    qrows = rows // nd
    width, rpp = outbox.shape[3], outbox.shape[2]
    groups = tsend.shape[0]
    me_d, me_t = lax.axis_index("depth"), lax.axis_index("tile")
    mesh_ids = pl.DeviceIdType.MESH

    barrier = pltpu.get_barrier_semaphore()

    @pl.loop(1, nt)
    def _(o):
        pl.semaphore_signal(barrier, inc=1, device_id=(me_d, lax.rem(me_t + o, nt)), device_id_type=mesh_ids)

    for k in range(1, nd):
        pl.semaphore_signal(barrier, inc=1, device_id=(lax.rem(me_d + k, nd), me_t), device_id_type=mesh_ids)

    def cols_of(b):
        return pl.ds(pl.multiple_of(b * CB, CB), CB)

    def pads_of(b):
        return pl.ds(pl.multiple_of(b * CB + PAD, PAD), CB)

    def dens_copy(b):
        return pltpu.make_async_copy(
            dens.at[:, :, cols_of(b)], d.at[pl.ds(1, cells), pl.ds(0, rows), pads_of(b)], dens_sem.at[b])

    def halo(kind, b):
        inner = pl.ds(1, cells)
        src, dst, step = (
            (dens.at[cells - 1, :, cols_of(b)], d.at[0, pl.ds(0, rows), pads_of(b)], 1),
            (dens.at[0, :, cols_of(b)], d.at[cells + 1, pl.ds(0, rows), pads_of(b)], nd - 1),
            (dens.at[:, pl.ds(rows - EDGE, EDGE), cols_of(b)],
             d.at[inner, pl.ds(rows, EDGE), pads_of(b)], 1),
            (dens.at[:, pl.ds(0, EDGE), cols_of(b)],
             d.at[inner, pl.ds(rows + EDGE, EDGE), pads_of(b)], nt - 1),
        )[kind]
        to = (lax.rem(me_d + step, nd), me_t) if kind < 2 else (me_d, lax.rem(me_t + step, nt))
        return pltpu.make_async_remote_copy(
            src_ref=src, dst_ref=dst, send_sem=hsend.at[kind, b], recv_sem=hrecv.at[kind, b],
            device_id=to, device_id_type=mesh_ids)

    sends = (me_d < nd - 1, me_d > 0, me_t < nt - 1, me_t > 0)
    gets = (me_d > 0, me_d < nd - 1, me_t > 0, me_t < nt - 1)

    @pl.loop(0, nb)
    def _(b):
        dens_copy(b).start()

    side = jnp.zeros((cells + 2, rows + 2 * EDGE, PAD), d.dtype)
    d[:, :, :PAD] = side
    d[:, :, cols + PAD:] = side

    @pl.when(me_d == 0)
    def _():
        d[0, 0:rows, PAD:cols + PAD] = jnp.zeros((rows, cols), d.dtype)

    @pl.when(me_d == nd - 1)
    def _():
        d[cells + 1, 0:rows, PAD:cols + PAD] = jnp.zeros((rows, cols), d.dtype)

    edge = jnp.zeros((cells, EDGE, cols), d.dtype)

    @pl.when(me_t == 0)
    def _():
        d[1:cells + 1, rows:rows + EDGE, PAD:cols + PAD] = edge

    @pl.when(me_t == nt - 1)
    def _():
        d[1:cells + 1, rows + EDGE:, PAD:cols + PAD] = edge

    pl.semaphore_wait(barrier, nt - 1 + nd - 1)

    @pl.loop(0, nb)
    def _(b):
        for kind in range(4):
            @pl.when(sends[kind])
            def _():
                halo(kind, b).start()

    def label_copy(o):
        return pltpu.make_async_remote_copy(
            src_ref=names, dst_ref=arrived.at[o], send_sem=lsend.at[o], recv_sem=lrecv.at[o],
            device_id=(me_d, lax.rem(me_t + o, nt)), device_id_type=mesh_ids)

    own_labels = pltpu.make_async_copy(names, arrived.at[0], lsend.at[0])
    own_labels.start()

    @pl.loop(1, nt)
    def _(o):
        label_copy(o).start()

    @pl.loop(0, nt)
    def _(o):
        start = lax.rem(me_t + o, nt) * ppd
        first, last = ppd - 1, 0
        for p in range(ppd):
            h = home[p] - start
            hit = (h >= 0) & (h < ppd)
            first = jnp.where(hit, jnp.minimum(first, p), first)
            last = jnp.where(hit, p, last)
        route[o, 0] = first
        route[o, 1] = last

    def arrive(b):
        dens_copy(b).wait()

    def arrive_halo(b):
        for kind in range(4):
            @pl.when(gets[kind])
            def _():
                halo(kind, b).wait_recv()

    ascend = rank[0] == 0
    across, begin, end = make_facing(d, g, dens16, left, right, rows, zc)

    def depth_copy(k, b, src):
        to = lax.rem(me_d + k, nd)
        return pltpu.make_async_remote_copy(
            src_ref=out.at[:, pl.ds(pl.multiple_of(to * qrows, 8), qrows), cols_of(b)],
            dst_ref=recv.at[src, :, :, cols_of(b)],
            send_sem=dsend.at[b, k], recv_sem=drecv.at[b, src],
            device_id=(to, me_t), device_id_type=mesh_ids)

    def keep_own(b):
        mine = out[:, pl.ds(pl.multiple_of(me_d * qrows, 8), qrows), cols_of(b)]
        recv[me_d, :, :, cols_of(b)] = mine

    def brick(i, b):
        one, two = recv[i, 0, :, cols_of(b)], recv[i, 1, :, cols_of(b)]
        colors = jnp.stack([low_part(one), high_part(one), low_part(two)])
        return colors, high_part(two) * (1.0 / UNIT)

    def composite(b):
        for k in range(1, nd):
            depth_copy(k, b, lax.rem(me_d + k, nd)).wait_recv()
        color, trans = brick(0, b)
        for i in range(1, nd):
            new, new_trans = brick(i, b)
            front, back = jnp.where(ascend, color, new), jnp.where(ascend, new, color)
            color = front + jnp.where(ascend, trans, new_trans)[None] * back
            trans = trans * new_trans
        for ch in range(3):
            fin[ch, :, cols_of(b)] = coded(color[ch] + trans * (BACKDROP[ch] * UNIT))

    def tile_copy(o, part, window):
        return pltpu.make_async_remote_copy(
            src_ref=outbox.at[o, :, :, window], dst_ref=inbox.at[o, :, :, window],
            send_sem=tsend.at[part, o], recv_sem=trecv.at[part, o],
            device_id=(me_d, lax.rem(me_t + o, nt)), device_id_type=mesh_ids)

    def tile_own(part, window):
        return pltpu.make_async_copy(
            outbox.at[0, :, :, window], inbox.at[0, :, :, window], tsend.at[part, 0])

    def ship(part, window):
        def piece(p, r):
            if width == cols:
                return fin[:, pl.ds(p * rpp + r, 1), window]
            per = cols // width
            c = pl.multiple_of(lax.rem(p, per) * width, width)
            return fin[:, pl.ds(lax.div(p, per), 1), pl.ds(c, width)]

        @pl.loop(0, nt)
        def _(o):
            for r in range(rpp):
                outbox[o, :, r:r + 1, window] = join(piece(route[o, 0], r), piece(route[o, 1], r))

        tile_own(part, window).start()

        @pl.loop(1, nt)
        def _(o):
            tile_copy(o, part, window).start()

    arrive(0)
    arrive(1)
    arrive_halo(0)

    @pl.loop(0, nd)
    def _(it):
        dx = across(0, it)
        for i in range(zc):
            end(0, 0, it, i, dx, begin(0, it, i))

    def finish(b):
        composite(b)
        if groups == nb:
            ship(b, cols_of(b))

    @pl.loop(0, nb)
    def _(b):
        slot = lax.rem(b, 2)

        @pl.when(b + 2 < nb)
        def _():
            arrive(b + 2)

        @pl.when(b + 1 < nb)
        def _():
            arrive_halo(b + 1)

        ahead = lax.rem(b + 1, nb)

        @pl.loop(0, nd)
        def _(it):
            k = it + 1
            band = pl.multiple_of(lax.rem(me_d + k, nd) * qrows, 8)
            beside = Beside(parts * cells, zc, lambda: across(ahead, it), lambda i: begin(ahead, it, i),
                            lambda i, dx, dyz: end(ahead, 1 - slot, it, i, dx, dyz))
            for part in range(parts):
                vals = march(dens16, g, slot, ascend, band, slice(part * MC, (part + 1) * MC), qrows, cells,
                             lambda step, first=part * cells: beside(first + step))
                c0, c1, c2, tr = (coded(val * UNIT) for val in vals)
                lanes = pl.ds(pl.multiple_of(b * CB + part * MC, MC), MC)
                out[0, pl.ds(band, qrows), lanes] = join(c0, c1)
                out[1, pl.ds(band, qrows), lanes] = join(c2, tr)
            beside(parts * cells)

            @pl.when(k < nd)
            def _():
                depth_copy(k, b, me_d).start()

        keep_own(b)

        @pl.when(b > 0)
        def _():
            finish(b - 1)

    finish(nb - 1)
    if groups != nb:
        ship(0, pl.ds(0, width))

    own_labels.wait()

    @pl.loop(1, nt)
    def _(o):
        label_copy(o).wait()

    @pl.loop(0, groups)
    def _(part):
        window = cols_of(part) if groups == nb else pl.ds(0, width)
        tile_own(part, window).wait()

        @pl.loop(1, nt)
        def _(o):
            tile_copy(o, part, window).wait()

    @pl.loop(0, nb)
    def _(b):
        for k in range(1, nd):
            depth_copy(k, b, me_d).wait_send()

    for kind in range(4):
        @pl.when(sends[kind])
        def _():
            @pl.loop(0, nb)
            def _(b):
                halo(kind, b).wait_send()


def place_kernel(arrived, inbox, display):
    nt, rpp, width = inbox.shape[0], inbox.shape[2], inbox.shape[3]
    ppd = display.shape[2]
    start = lax.axis_index("tile") * ppd

    @pl.loop(0, nt)
    def _(o):
        first, last = jnp.int32(NONE), jnp.int32(NONE)
        for p in range(ppd):
            h = arrived[o, 0, p] - start
            hit = (h >= 0) & (h < ppd)
            first = jnp.where(hit & (first == NONE), h, first)
            last = jnp.where(hit, h, last)

        def put(label, part):
            for r in range(rpp):
                piece = part(inbox[o, :, r:r + 1, :]) * (1.0 / UNIT)
                display[:, 0, pl.ds(label, 1), r * width:(r + 1) * width] = piece

        @pl.when(first != NONE)
        def _():
            put(first, low_part)

        @pl.when(last != first)
        def _():
            put(last, high_part)


def on_device(density, depth_rank, piece_home):
    cells, rows, cols = density.shape
    nd, nt = lax.axis_size("depth"), lax.axis_size("tile")
    ppd = piece_home.shape[0]
    qrows = rows // nd
    piece_len = qrows * cols // ppd
    width = min(piece_len, cols)
    rpp = piece_len // width
    nb = cols // CB
    groups = nb if width == cols else 1

    names = piece_home.reshape(1, ppd)
    left, right = stencils(rows)
    anyspec = pl.BlockSpec(memory_space=pl.ANY)
    vmem = pl.BlockSpec(memory_space=pltpu.VMEM)
    smem = pl.BlockSpec(memory_space=pltpu.SMEM)
    dma = pltpu.SemaphoreType.DMA
    f32, i32 = jnp.float32, jnp.int32
    inbox, arrived = pl.pallas_call(
        lambda *refs: brick_kernel(nd, nt, ppd, *refs),
        out_shape=(jax.ShapeDtypeStruct((nt, 3, rpp, width), i32),
                   jax.ShapeDtypeStruct((nt, 1, ppd), i32)),
        in_specs=[smem, smem] + [anyspec] * 2 + [vmem] * 2,
        out_specs=(anyspec, anyspec),
        scratch_shapes=[
            pltpu.VMEM((cells + 2, rows + 2 * EDGE, cols + 2 * PAD), jnp.bfloat16),
            pltpu.VMEM((2, cells, rows, CB), f32),
            pltpu.VMEM((2, cells, rows, CB), jnp.bfloat16),
            pltpu.VMEM((2, rows, cols), i32),
            pltpu.VMEM((nd, 2, qrows, cols), i32),
            pltpu.VMEM((3, qrows, cols), i32),
            pltpu.VMEM((nt, 3, rpp, width), i32),
            pltpu.SMEM((nt, MOST), i32),
            dma((nb,)), dma((4, nb)), dma((4, nb)), dma((nb, nd)), dma((nb, nd)),
            dma((groups, nt)), dma((groups, nt)), dma((nt,)), dma((nt,)),
        ],
        compiler_params=pltpu.CompilerParams(
            collective_id=0, has_side_effects=True, vmem_limit_bytes=56 * 1024 * 1024),
    )(depth_rank, piece_home, density, names, left, right)
    return pl.pallas_call(
        place_kernel,
        out_shape=jax.ShapeDtypeStruct((3, 1, ppd, piece_len), f32),
        in_specs=[smem, vmem],
        out_specs=vmem,
    )(arrived, inbox)


def solution(mesh):
    in_specs = (P("depth", "tile", None), P(), P("tile"))
    out_specs = P(None, "depth", "tile", None)
    return jax.shard_map(
        on_device, mesh=mesh, in_specs=in_specs, out_specs=out_specs, check_vma=False
    )
```

```python
import math
import jax
import jax.numpy as jnp
import numpy as np
from jax import lax
from jax.experimental import pallas as pl
from jax.experimental.pallas import tpu as pltpu
from jax.sharding import PartitionSpec as P

MOST = 2
NONE = -1

EXTINCT = 0.5
LIGHT_Z = 0.6
LIGHT_Y = 0.48
LIGHT_X = 0.64
SHARPNESS = 6.0
BACKDROP = (0.08, 0.1, 0.14)

PAD = 128
CB = 256
MC = 128
EDGE = 8
SIG_A = math.exp(-3.0)
SIG_B = math.exp(-2.5)
SHIFT = math.pi / 2 / (0.85 * math.log(2))
LEAD = 6.138231308051623e-10
SINSQ = (141379137.46788317, -4089655.3240788155, 47304.237438791075, -291.0939487912164)
UNIT = 65535.0
LOW = 65535


def stencils(rows):
    wy, wz = LIGHT_Y / LIGHT_X, LIGHT_Z / LIGHT_X
    left = np.zeros((rows, 3 * rows + 2 * EDGE), np.float32)
    for r in range(rows):
        left[r, r] = -wz
        left[r, 2 * rows + 2 * EDGE + r] = wz
        if r < rows - 1:
            left[r, rows + r + 1] = wy
        if r > 0:
            left[r, rows + r - 1] = -wy
    left[0, 2 * rows + EDGE - 1] = -wy
    left[rows - 1, 2 * rows + EDGE] = wy
    right = np.zeros((CB + 2 * PAD, CB), np.float32)
    for c in range(CB):
        right[c + PAD + 1, c] = 1.0
        right[c + PAD - 1, c] = -1.0
    plain = np.delete(left, np.s_[2 * rows:2 * rows + 2 * EDGE], axis=1)
    return [jnp.asarray(m, jnp.bfloat16) for m in (left, plain, right)]


def make_facing(d, g, dens16, left, plain, right, rows, cells, zc):
    def across(block, chunk):
        wide = d[pl.ds(chunk * zc + 1, zc), 0:rows, pl.ds(pl.multiple_of(block * CB, CB), CB + 2 * PAD)]
        wide = wide.reshape(zc * rows, CB + 2 * PAD)
        return [jnp.dot(wide[:, h:h + CB], right[h:h + CB], preferred_element_type=jnp.float32)
                for h in range(0, CB + 2 * PAD, CB)]

    def begin(block, chunk, i):
        z = chunk * zc + i
        c1 = pl.multiple_of(block * CB + PAD, PAD)
        tall = jnp.concatenate([
            d[z, 0:rows, pl.ds(c1, CB)],
            d[z + 1, :, pl.ds(c1, CB)],
            d[z + 2, 0:rows, pl.ds(c1, CB)]], axis=0)
        return jnp.dot(left[...], tall, preferred_element_type=jnp.float32)

    def end(block, slot, chunk, i, dx, dyz):
        z = chunk * zc + i
        g[slot, z] = dyz + sum(part[i * rows:(i + 1) * rows] for part in dx)
        dens16[slot, z] = d[z + 1, 0:rows, pl.ds(pl.multiple_of(block * CB + PAD, PAD), CB)]

    def inner(block, z):
        c1 = pl.multiple_of(block * CB + PAD, PAD)
        tall = d[pl.ds(z, 3), 0:rows, pl.ds(c1, CB)].reshape(3 * rows, CB)
        wide = d[z + 1, 0:rows, pl.ds(pl.multiple_of(block * CB, CB), CB + 2 * PAD)]
        dx = jnp.dot(wide, right[...], preferred_element_type=jnp.float32)
        g[0, z] = jnp.dot(plain[...], tall, preferred_element_type=jnp.float32) + dx
        dens16[0, z] = d[z + 1, 0:rows, pl.ds(c1, CB)]

    def early(block):
        @pl.loop(0, cells // 2 - 1)
        def _(i):
            for j in range(2):
                inner(block, 2 * i + 1 + j)

    def late(block):
        wy = LIGHT_Y / LIGHT_X
        c1 = pl.multiple_of(block * CB + PAD, PAD)
        for z in (0, cells - 1):
            inner(block, z)

        @pl.loop(0, cells // 4)
        def _(i):
            sub = lax.broadcasted_iota(jnp.int32, (EDGE, CB), 0)
            for j in range(4):
                z = 4 * i + j
                low = d[z + 1, rows:rows + EDGE, pl.ds(c1, CB)].astype(jnp.float32)
                high = d[z + 1, rows + EDGE:, pl.ds(c1, CB)].astype(jnp.float32)
                g[0, z, 0:EDGE] = g[0, z, 0:EDGE] - jnp.where(sub == 0, pltpu.roll(low, 1, 0), 0.0) * wy
                g[0, z, rows - EDGE:] = g[0, z, rows - EDGE:] + jnp.where(
                    sub == EDGE - 1, pltpu.roll(high, EDGE - 1, 0), 0.0) * wy

    return across, begin, end, early, late


def march(dens16, g, slot, ascend, r0, lanes, band_rows, cells, beside):
    bias = (0.35 + 0.65 * 0.5) / (0.65 * 0.5)
    zero = jnp.zeros((band_rows, MC), jnp.float32)
    trans = zero + 1.0
    total = m0 = m1 = wave = zero
    for k in range(cells):
        beside(k)
        z = jnp.where(ascend, k, cells - 1 - k)
        dens = dens16[slot, z, pl.ds(r0, band_rows), lanes].astype(jnp.float32)
        face = g[slot, z, pl.ds(r0, band_rows), lanes]
        shade = jnp.tanh(face * (0.5 * SHARPNESS * LIGHT_X)) + bias
        after = trans * jnp.exp2(dens * (-EXTINCT * math.log2(math.e)))
        ws = (trans - after) * shade
        trans = after
        v = jnp.log2(dens + 0.01) + SHIFT
        q = v * v
        c = q + SINSQ[-1]
        for coef in SINSQ[-2::-1]:
            c = c * q + coef
        c = c * q
        total = total + ws
        m0 = m0 + ws * (1.0 / (dens + (0.01 + SIG_A)))
        m1 = m1 + ws * (1.0 / (dens + (0.01 + SIG_B)))
        wave = wave + ws * (c * (1.0 / LEAD - c))
    scale = 0.65 * 0.5
    return (
        scale * (total - SIG_A * m0),
        (scale * 4 * LEAD * LEAD) * wave,
        (scale * SIG_B) * m1,
        trans,
    )


class Beside:
    def __init__(self, steps, planes, across, begin, end):
        self.across, self.begin, self.end = across, begin, end
        gap = steps // planes
        self.turns = {}
        for i in range(planes):
            self.turns.setdefault(i * gap, []).append((True, i))
            stop = min(i * gap + gap * 24 // 8, steps)
            self.turns.setdefault(stop, []).append((False, i))
        self.held, self.dx = {}, None

    def __call__(self, step):
        if step == 0:
            self.dx = self.across()
        for fresh, i in self.turns.get(step, ()):
            if fresh:
                self.held[i] = self.begin(i)
            else:
                self.end(i, self.dx, self.held[i])


def coded(value):
    return jnp.clip(value + 0.5, 0.0, UNIT).astype(jnp.int32)


def join(low, high):
    return low | (high << 16)


def low_part(word):
    return (word & LOW).astype(jnp.float32)


def high_part(word):
    return lax.shift_right_logical(word, 16).astype(jnp.float32)


def brick_kernel(nd, nt, ppd, rank, home, dens, names, left, plain, right, inbox, arrived,
                 d, g, dens16, out, recv, fin, outbox, route,
                 dens_sem, hsend, hrecv, dsend, drecv, tsend, trecv, lsend, lrecv):
    cells, rows, cols = dens.shape
    nb, parts = cols // CB, CB // MC
    zc = cells // nd
    qrows = rows // nd
    width, rpp = outbox.shape[3], outbox.shape[2]
    groups = tsend.shape[0]
    me_d, me_t = lax.axis_index("depth"), lax.axis_index("tile")
    mesh_ids = pl.DeviceIdType.MESH

    barrier = pltpu.get_barrier_semaphore()

    @pl.loop(1, nt)
    def _(o):
        pl.semaphore_signal(barrier, inc=1, device_id=(me_d, lax.rem(me_t + o, nt)), device_id_type=mesh_ids)

    for k in range(1, nd):
        pl.semaphore_signal(barrier, inc=1, device_id=(lax.rem(me_d + k, nd), me_t), device_id_type=mesh_ids)

    def cols_of(b):
        return pl.ds(pl.multiple_of(b * CB, CB), CB)

    def pads_of(b):
        return pl.ds(pl.multiple_of(b * CB + PAD, PAD), CB)

    def dens_copy(b):
        return pltpu.make_async_copy(
            dens.at[:, :, cols_of(b)], d.at[pl.ds(1, cells), pl.ds(0, rows), pads_of(b)], dens_sem.at[b])

    def halo(kind, b):
        inner = pl.ds(1, cells)
        src, dst, step = (
            (dens.at[cells - 1, :, cols_of(b)], d.at[0, pl.ds(0, rows), pads_of(b)], 1),
            (dens.at[0, :, cols_of(b)], d.at[cells + 1, pl.ds(0, rows), pads_of(b)], nd - 1),
            (dens.at[:, pl.ds(rows - EDGE, EDGE), cols_of(b)],
             d.at[inner, pl.ds(rows, EDGE), pads_of(b)], 1),
            (dens.at[:, pl.ds(0, EDGE), cols_of(b)],
             d.at[inner, pl.ds(rows + EDGE, EDGE), pads_of(b)], nt - 1),
        )[kind]
        to = (lax.rem(me_d + step, nd), me_t) if kind < 2 else (me_d, lax.rem(me_t + step, nt))
        return pltpu.make_async_remote_copy(
            src_ref=src, dst_ref=dst, send_sem=hsend.at[kind, b], recv_sem=hrecv.at[kind, b],
            device_id=to, device_id_type=mesh_ids)

    sends = (me_d < nd - 1, me_d > 0, me_t < nt - 1, me_t > 0)
    gets = (me_d > 0, me_d < nd - 1, me_t > 0, me_t < nt - 1)

    for b in range(2):
        dens_copy(b).start()

    side = jnp.zeros((cells + 2, rows + 2 * EDGE, PAD), d.dtype)
    d[:, :, :PAD] = side
    d[:, :, cols + PAD:] = side

    @pl.when(me_d == 0)
    def _():
        d[0, 0:rows, PAD:cols + PAD] = jnp.zeros((rows, cols), d.dtype)

    @pl.when(me_d == nd - 1)
    def _():
        d[cells + 1, 0:rows, PAD:cols + PAD] = jnp.zeros((rows, cols), d.dtype)

    edge = jnp.zeros((cells, EDGE, cols), d.dtype)

    @pl.when(me_t == 0)
    def _():
        d[1:cells + 1, rows:rows + EDGE, PAD:cols + PAD] = edge

    @pl.when(me_t == nt - 1)
    def _():
        d[1:cells + 1, rows + EDGE:, PAD:cols + PAD] = edge

    pl.semaphore_wait(barrier, nt - 1 + nd - 1)

    def send_halo(b):
        for kind in range(4):
            @pl.when(sends[kind])
            def _():
                halo(kind, b).start()

    send_halo(0)
    dens_copy(2).start()
    dens_copy(3).start()
    send_halo(1)

    def label_copy(o):
        return pltpu.make_async_remote_copy(
            src_ref=names, dst_ref=arrived.at[o], send_sem=lsend.at[o], recv_sem=lrecv.at[o],
            device_id=(me_d, lax.rem(me_t + o, nt)), device_id_type=mesh_ids)

    own_labels = pltpu.make_async_copy(names, arrived.at[0], lsend.at[0])
    own_labels.start()

    @pl.loop(1, nt)
    def _(o):
        label_copy(o).start()

    @pl.loop(0, nt)
    def _(o):
        start = lax.rem(me_t + o, nt) * ppd
        first, last = ppd - 1, 0
        for p in range(ppd):
            h = home[p] - start
            hit = (h >= 0) & (h < ppd)
            first = jnp.where(hit, jnp.minimum(first, p), first)
            last = jnp.where(hit, p, last)
        route[o, 0] = first
        route[o, 1] = last

    def arrive(b):
        dens_copy(b).wait()

    def arrive_halo(b):
        for kind in range(4):
            @pl.when(gets[kind])
            def _():
                halo(kind, b).wait_recv()

    ascend = rank[0] == 0
    across, begin, end, early, late = make_facing(d, g, dens16, left, plain, right, rows, cells, zc)

    def depth_copy(k, b, src):
        to = lax.rem(me_d + k, nd)
        return pltpu.make_async_remote_copy(
            src_ref=out.at[:, pl.ds(pl.multiple_of(to * qrows, 8), qrows), cols_of(b)],
            dst_ref=recv.at[src, :, :, cols_of(b)],
            send_sem=dsend.at[b, k], recv_sem=drecv.at[b, src],
            device_id=(to, me_t), device_id_type=mesh_ids)

    def keep_own(b):
        mine = out[:, pl.ds(pl.multiple_of(me_d * qrows, 8), qrows), cols_of(b)]
        recv[me_d, :, :, cols_of(b)] = mine

    def brick(i, b):
        one, two = recv[i, 0, :, cols_of(b)], recv[i, 1, :, cols_of(b)]
        colors = jnp.stack([low_part(one), high_part(one), low_part(two)])
        return colors, high_part(two) * (1.0 / UNIT)

    def composite(b):
        for k in range(1, nd):
            depth_copy(k, b, lax.rem(me_d + k, nd)).wait_recv()
        color, trans = brick(0, b)
        for i in range(1, nd):
            new, new_trans = brick(i, b)
            front, back = jnp.where(ascend, color, new), jnp.where(ascend, new, color)
            color = front + jnp.where(ascend, trans, new_trans)[None] * back
            trans = trans * new_trans
        for ch in range(3):
            fin[ch, :, cols_of(b)] = coded(color[ch] + trans * (BACKDROP[ch] * UNIT))

    def tile_copy(o, part, window):
        return pltpu.make_async_remote_copy(
            src_ref=outbox.at[o, :, :, window], dst_ref=inbox.at[o, :, :, window],
            send_sem=tsend.at[part, o], recv_sem=trecv.at[part, o],
            device_id=(me_d, lax.rem(me_t + o, nt)), device_id_type=mesh_ids)

    def tile_own(part, window):
        return pltpu.make_async_copy(
            outbox.at[0, :, :, window], inbox.at[0, :, :, window], tsend.at[part, 0])

    def ship(part, window):
        def piece(p, r):
            if width == cols:
                return fin[:, pl.ds(p * rpp + r, 1), window]
            per = cols // width
            c = pl.multiple_of(lax.rem(p, per) * width, width)
            return fin[:, pl.ds(lax.div(p, per), 1), pl.ds(c, width)]

        @pl.loop(0, nt)
        def _(o):
            for r in range(rpp):
                outbox[o, :, r:r + 1, window] = join(piece(route[o, 0], r), piece(route[o, 1], r))

        tile_own(part, window).start()

        @pl.loop(1, nt)
        def _(o):
            tile_copy(o, part, window).start()

    arrive(0)
    arrive(1)
    early(0)
    arrive_halo(0)
    late(0)

    def finish(b):
        composite(b)
        if groups == nb:
            ship(b, cols_of(b))

    def block(b, beside_of):
        slot = lax.rem(b, 2)

        if isinstance(b, int):
            assert b == nb - 1
        else:
            @pl.when(b + 4 < nb)
            def _():
                dens_copy(b + 4).start()

            @pl.when(b + 2 < nb)
            def _():
                send_halo(b + 2)
                arrive(b + 2)

            arrive_halo(b + 1)

        @pl.loop(0, nd)
        def _(it):
            k = it + 1
            band = pl.multiple_of(lax.rem(me_d + k, nd) * qrows, 8)
            beside = beside_of(b + 1, 1 - slot, it)
            for part in range(parts):
                vals = march(dens16, g, slot, ascend, band, slice(part * MC, (part + 1) * MC), qrows, cells,
                             lambda step, first=part * cells: beside(first + step))
                c0, c1, c2, tr = (coded(val * UNIT) for val in vals)
                lanes = pl.ds(pl.multiple_of(b * CB + part * MC, MC), MC)
                out[0, pl.ds(band, qrows), lanes] = join(c0, c1)
                out[1, pl.ds(band, qrows), lanes] = join(c2, tr)
            beside(parts * cells)

            @pl.when(k < nd)
            def _():
                depth_copy(k, b, me_d).start()

        keep_own(b)

        @pl.when(b > 0)
        def _():
            finish(b - 1)

    def slopes_of(ahead, slot, it):
        return Beside(parts * cells, zc, lambda: across(ahead, it), lambda i: begin(ahead, it, i),
                      lambda i, dx, dyz: end(ahead, slot, it, i, dx, dyz))

    @pl.loop(0, nb - 1)
    def _(b):
        block(b, slopes_of)

    block(nb - 1, lambda ahead, slot, it: lambda step: None)
    finish(nb - 1)
    if groups != nb:
        ship(0, pl.ds(0, width))

    own_labels.wait()

    @pl.loop(1, nt)
    def _(o):
        label_copy(o).wait()

    @pl.loop(0, groups)
    def _(part):
        window = cols_of(part) if groups == nb else pl.ds(0, width)
        tile_own(part, window).wait()

        @pl.loop(1, nt)
        def _(o):
            tile_copy(o, part, window).wait()

    @pl.loop(0, nb)
    def _(b):
        for k in range(1, nd):
            depth_copy(k, b, me_d).wait_send()

    for kind in range(4):
        @pl.when(sends[kind])
        def _():
            @pl.loop(0, nb)
            def _(b):
                halo(kind, b).wait_send()


def place_kernel(arrived, inbox, display):
    nt, rpp, width = inbox.shape[0], inbox.shape[2], inbox.shape[3]
    ppd = display.shape[2]
    start = lax.axis_index("tile") * ppd

    @pl.loop(0, nt)
    def _(o):
        first, last = jnp.int32(NONE), jnp.int32(NONE)
        for p in range(ppd):
            h = arrived[o, 0, p] - start
            hit = (h >= 0) & (h < ppd)
            first = jnp.where(hit & (first == NONE), h, first)
            last = jnp.where(hit, h, last)

        def put(label, part):
            for r in range(rpp):
                piece = part(inbox[o, :, r:r + 1, :]) * (1.0 / UNIT)
                display[:, 0, pl.ds(label, 1), r * width:(r + 1) * width] = piece

        @pl.when(first != NONE)
        def _():
            put(first, low_part)

        @pl.when(last != first)
        def _():
            put(last, high_part)


def on_device(density, depth_rank, piece_home):
    cells, rows, cols = density.shape
    nd, nt = lax.axis_size("depth"), lax.axis_size("tile")
    ppd = piece_home.shape[0]
    qrows = rows // nd
    piece_len = qrows * cols // ppd
    width = min(piece_len, cols)
    rpp = piece_len // width
    nb = cols // CB
    groups = nb if width == cols else 1

    names = piece_home.reshape(1, ppd)
    left, plain, right = stencils(rows)
    anyspec = pl.BlockSpec(memory_space=pl.ANY)
    vmem = pl.BlockSpec(memory_space=pltpu.VMEM)
    smem = pl.BlockSpec(memory_space=pltpu.SMEM)
    dma = pltpu.SemaphoreType.DMA
    f32, i32 = jnp.float32, jnp.int32
    inbox, arrived = pl.pallas_call(
        lambda *refs: brick_kernel(nd, nt, ppd, *refs),
        out_shape=(jax.ShapeDtypeStruct((nt, 3, rpp, width), i32),
                   jax.ShapeDtypeStruct((nt, 1, ppd), i32)),
        in_specs=[smem, smem] + [anyspec] * 2 + [vmem] * 3,
        out_specs=(anyspec, anyspec),
        scratch_shapes=[
            pltpu.VMEM((cells + 2, rows + 2 * EDGE, cols + 2 * PAD), jnp.bfloat16),
            pltpu.VMEM((2, cells, rows, CB), f32),
            pltpu.VMEM((2, cells, rows, CB), jnp.bfloat16),
            pltpu.VMEM((2, rows, cols), i32),
            pltpu.VMEM((nd, 2, qrows, cols), i32),
            pltpu.VMEM((3, qrows, cols), i32),
            pltpu.VMEM((nt, 3, rpp, width), i32),
            pltpu.SMEM((nt, MOST), i32),
            dma((nb,)), dma((4, nb)), dma((4, nb)), dma((nb, nd)), dma((nb, nd)),
            dma((groups, nt)), dma((groups, nt)), dma((nt,)), dma((nt,)),
        ],
        compiler_params=pltpu.CompilerParams(
            collective_id=0, has_side_effects=True, vmem_limit_bytes=56 * 1024 * 1024),
    )(depth_rank, piece_home, density, names, left, plain, right)
    return pl.pallas_call(
        place_kernel,
        out_shape=jax.ShapeDtypeStruct((3, 1, ppd, piece_len), f32),
        in_specs=[smem, vmem],
        out_specs=vmem,
    )(arrived, inbox)


def solution(mesh):
    in_specs = (P("depth", "tile", None), P(), P("tile"))
    out_specs = P(None, "depth", "tile", None)
    return jax.shard_map(
        on_device, mesh=mesh, in_specs=in_specs, out_specs=out_specs, check_vma=False
    )
```

```python
import math
import jax
import jax.numpy as jnp
import numpy as np
from jax import lax
from jax.experimental import pallas as pl
from jax.experimental.pallas import tpu as pltpu
from jax.sharding import PartitionSpec as P

MOST = 2
NONE = -1

EXTINCT = 0.5
LIGHT_Z = 0.6
LIGHT_Y = 0.48
LIGHT_X = 0.64
SHARPNESS = 6.0
BACKDROP = (0.08, 0.1, 0.14)

PAD = 128
CB = 256
MC = 128
EDGE = 8
SIG_A = math.exp(-3.0)
SIG_B = math.exp(-2.5)
SHIFT = math.pi / 2 / (0.85 * math.log(2))
LEAD = 6.138231308051623e-10
SINSQ = (141379137.46788317, -4089655.3240788155, 47304.237438791075, -291.0939487912164)
UNIT = 65535.0
LOW = 65535


def stencils(rows):
    wy, wz = LIGHT_Y / LIGHT_X, LIGHT_Z / LIGHT_X
    left = np.zeros((rows, 3 * rows + 2 * EDGE), np.float32)
    for r in range(rows):
        left[r, r] = -wz
        left[r, 2 * rows + 2 * EDGE + r] = wz
        if r < rows - 1:
            left[r, rows + r + 1] = wy
        if r > 0:
            left[r, rows + r - 1] = -wy
    left[0, 2 * rows + EDGE - 1] = -wy
    left[rows - 1, 2 * rows + EDGE] = wy
    right = np.zeros((CB + 2 * PAD, CB), np.float32)
    for c in range(CB):
        right[c + PAD + 1, c] = 1.0
        right[c + PAD - 1, c] = -1.0
    plain = np.delete(left, np.s_[2 * rows:2 * rows + 2 * EDGE], axis=1)
    return [jnp.asarray(m, jnp.bfloat16) for m in (left, plain, right)]


def make_facing(d, g, dens16, left, plain, right, rows, cells, zc):
    def across(block, chunk):
        wide = d[pl.ds(chunk * zc + 1, zc), 0:rows, pl.ds(pl.multiple_of(block * CB, CB), CB + 2 * PAD)]
        wide = wide.reshape(zc * rows, CB + 2 * PAD)
        return [jnp.dot(wide[:, h:h + CB], right[h:h + CB], preferred_element_type=jnp.float32)
                for h in range(0, CB + 2 * PAD, CB)]

    def begin(block, chunk, i):
        z = chunk * zc + i
        c1 = pl.multiple_of(block * CB + PAD, PAD)
        tall = jnp.concatenate([
            d[z, 0:rows, pl.ds(c1, CB)],
            d[z + 1, :, pl.ds(c1, CB)],
            d[z + 2, 0:rows, pl.ds(c1, CB)]], axis=0)
        return jnp.dot(left[...], tall, preferred_element_type=jnp.float32)

    def end(block, slot, chunk, i, dx, dyz):
        z = chunk * zc + i
        g[slot, z] = dyz + sum(part[i * rows:(i + 1) * rows] for part in dx)
        dens16[slot, z] = d[z + 1, 0:rows, pl.ds(pl.multiple_of(block * CB + PAD, PAD), CB)]

    def inner(block, z):
        c1 = pl.multiple_of(block * CB + PAD, PAD)
        tall = d[pl.ds(z, 3), 0:rows, pl.ds(c1, CB)].reshape(3 * rows, CB)
        wide = d[z + 1, 0:rows, pl.ds(pl.multiple_of(block * CB, CB), CB + 2 * PAD)]
        dx = jnp.dot(wide, right[...], preferred_element_type=jnp.float32)
        g[0, z] = jnp.dot(plain[...], tall, preferred_element_type=jnp.float32) + dx
        dens16[0, z] = d[z + 1, 0:rows, pl.ds(c1, CB)]

    def early(block):
        @pl.loop(0, cells // 2 - 1)
        def _(i):
            for j in range(2):
                inner(block, 2 * i + 1 + j)

    def late(block):
        wy = LIGHT_Y / LIGHT_X
        c1 = pl.multiple_of(block * CB + PAD, PAD)
        for z in (0, cells - 1):
            inner(block, z)

        @pl.loop(0, cells // 4)
        def _(i):
            sub = lax.broadcasted_iota(jnp.int32, (EDGE, CB), 0)
            for j in range(4):
                z = 4 * i + j
                low = d[z + 1, rows:rows + EDGE, pl.ds(c1, CB)].astype(jnp.float32)
                high = d[z + 1, rows + EDGE:, pl.ds(c1, CB)].astype(jnp.float32)
                g[0, z, 0:EDGE] = g[0, z, 0:EDGE] - jnp.where(sub == 0, pltpu.roll(low, 1, 0), 0.0) * wy
                g[0, z, rows - EDGE:] = g[0, z, rows - EDGE:] + jnp.where(
                    sub == EDGE - 1, pltpu.roll(high, EDGE - 1, 0), 0.0) * wy

    return across, begin, end, early, late


def march(dens16, g, slot, ascend, r0, lanes, band_rows, cells, beside):
    bias = (0.35 + 0.65 * 0.5) / (0.65 * 0.5)
    zero = jnp.zeros((band_rows, MC), jnp.float32)
    trans = zero + 1.0
    total = m0 = m1 = wave = zero
    for k in range(cells):
        beside(k)
        z = jnp.where(ascend, k, cells - 1 - k)
        dens = dens16[slot, z, pl.ds(r0, band_rows), lanes].astype(jnp.float32)
        face = g[slot, z, pl.ds(r0, band_rows), lanes]
        shade = jnp.tanh(face * (0.5 * SHARPNESS * LIGHT_X)) + bias
        after = trans * jnp.exp2(dens * (-EXTINCT * math.log2(math.e)))
        ws = (trans - after) * shade
        trans = after
        v = jnp.log2(dens + 0.01) + SHIFT
        q = v * v
        c = q + SINSQ[-1]
        for coef in SINSQ[-2::-1]:
            c = c * q + coef
        c = c * q
        total = total + ws
        m0 = m0 + ws * (1.0 / (dens + (0.01 + SIG_A)))
        m1 = m1 + ws * (1.0 / (dens + (0.01 + SIG_B)))
        wave = wave + ws * (c * (1.0 / LEAD - c))
    scale = 0.65 * 0.5
    return (
        scale * (total - SIG_A * m0),
        (scale * 4 * LEAD * LEAD) * wave,
        (scale * SIG_B) * m1,
        trans,
    )


class Beside:
    def __init__(self, steps, planes, across, begin, end):
        self.across, self.begin, self.end = across, begin, end
        gap = steps // planes
        self.turns = {}
        for i in range(planes):
            self.turns.setdefault(i * gap, []).append((True, i))
            stop = min(i * gap + gap * 32 // 8, steps)
            self.turns.setdefault(stop, []).append((False, i))
        self.held, self.dx = {}, None

    def __call__(self, step):
        if step == 0:
            self.dx = self.across()
        for fresh, i in self.turns.get(step, ()):
            if fresh:
                self.held[i] = self.begin(i)
            else:
                self.end(i, self.dx, self.held[i])


def coded(value):
    return jnp.clip(value + 0.5, 0.0, UNIT).astype(jnp.int32)


def join(low, high):
    return low | (high << 16)


def low_part(word):
    return (word & LOW).astype(jnp.float32)


def high_part(word):
    return lax.shift_right_logical(word, 16).astype(jnp.float32)


def brick_kernel(nd, nt, ppd, rank, home, dens, names, left, plain, right, inbox, arrived,
                 d, g, dens16, out, recv, fin, outbox, route,
                 dens_sem, hsend, hrecv, dsend, drecv, tsend, trecv, lsend, lrecv):
    cells, rows, cols = dens.shape
    nb, parts = cols // CB, CB // MC
    zc = cells // nd
    qrows = rows // nd
    width, rpp = outbox.shape[3], outbox.shape[2]
    groups = tsend.shape[0]
    me_d, me_t = lax.axis_index("depth"), lax.axis_index("tile")
    mesh_ids = pl.DeviceIdType.MESH

    barrier = pltpu.get_barrier_semaphore()

    @pl.loop(1, nt)
    def _(o):
        pl.semaphore_signal(barrier, inc=1, device_id=(me_d, lax.rem(me_t + o, nt)), device_id_type=mesh_ids)

    for k in range(1, nd):
        pl.semaphore_signal(barrier, inc=1, device_id=(lax.rem(me_d + k, nd), me_t), device_id_type=mesh_ids)

    def cols_of(b):
        return pl.ds(pl.multiple_of(b * CB, CB), CB)

    def pads_of(b):
        return pl.ds(pl.multiple_of(b * CB + PAD, PAD), CB)

    def dens_copy(b):
        return pltpu.make_async_copy(
            dens.at[:, :, cols_of(b)], d.at[pl.ds(1, cells), pl.ds(0, rows), pads_of(b)], dens_sem.at[b])

    def halo(kind, b):
        inner = pl.ds(1, cells)
        src, dst, step = (
            (dens.at[cells - 1, :, cols_of(b)], d.at[0, pl.ds(0, rows), pads_of(b)], 1),
            (dens.at[0, :, cols_of(b)], d.at[cells + 1, pl.ds(0, rows), pads_of(b)], nd - 1),
            (dens.at[:, pl.ds(rows - EDGE, EDGE), cols_of(b)],
             d.at[inner, pl.ds(rows, EDGE), pads_of(b)], 1),
            (dens.at[:, pl.ds(0, EDGE), cols_of(b)],
             d.at[inner, pl.ds(rows + EDGE, EDGE), pads_of(b)], nt - 1),
        )[kind]
        to = (lax.rem(me_d + step, nd), me_t) if kind < 2 else (me_d, lax.rem(me_t + step, nt))
        return pltpu.make_async_remote_copy(
            src_ref=src, dst_ref=dst, send_sem=hsend.at[kind, b], recv_sem=hrecv.at[kind, b],
            device_id=to, device_id_type=mesh_ids)

    sends = (me_d < nd - 1, me_d > 0, me_t < nt - 1, me_t > 0)
    gets = (me_d > 0, me_d < nd - 1, me_t > 0, me_t < nt - 1)

    for b in range(2):
        dens_copy(b).start()

    side = jnp.zeros((cells + 2, rows + 2 * EDGE, PAD), d.dtype)
    d[:, :, :PAD] = side
    d[:, :, cols + PAD:] = side

    @pl.when(me_d == 0)
    def _():
        d[0, 0:rows, PAD:cols + PAD] = jnp.zeros((rows, cols), d.dtype)

    @pl.when(me_d == nd - 1)
    def _():
        d[cells + 1, 0:rows, PAD:cols + PAD] = jnp.zeros((rows, cols), d.dtype)

    edge = jnp.zeros((cells, EDGE, cols), d.dtype)

    @pl.when(me_t == 0)
    def _():
        d[1:cells + 1, rows:rows + EDGE, PAD:cols + PAD] = edge

    @pl.when(me_t == nt - 1)
    def _():
        d[1:cells + 1, rows + EDGE:, PAD:cols + PAD] = edge

    pl.semaphore_wait(barrier, nt - 1 + nd - 1)

    def send_halo(b):
        for kind in range(4):
            @pl.when(sends[kind])
            def _():
                halo(kind, b).start()

    send_halo(0)
    dens_copy(2).start()
    dens_copy(3).start()
    send_halo(1)

    def label_copy(o):
        return pltpu.make_async_remote_copy(
            src_ref=names, dst_ref=arrived.at[o], send_sem=lsend.at[o], recv_sem=lrecv.at[o],
            device_id=(me_d, lax.rem(me_t + o, nt)), device_id_type=mesh_ids)

    own_labels = pltpu.make_async_copy(names, arrived.at[0], lsend.at[0])
    own_labels.start()

    @pl.loop(1, nt)
    def _(o):
        label_copy(o).start()

    @pl.loop(0, nt)
    def _(o):
        start = lax.rem(me_t + o, nt) * ppd
        first, last = ppd - 1, 0
        for p in range(ppd):
            h = home[p] - start
            hit = (h >= 0) & (h < ppd)
            first = jnp.where(hit, jnp.minimum(first, p), first)
            last = jnp.where(hit, p, last)
        route[o, 0] = first
        route[o, 1] = last

    def arrive(b):
        dens_copy(b).wait()

    def arrive_halo(b):
        for kind in range(4):
            @pl.when(gets[kind])
            def _():
                halo(kind, b).wait_recv()

    ascend = rank[0] == 0
    across, begin, end, early, late = make_facing(d, g, dens16, left, plain, right, rows, cells, zc)

    def depth_copy(k, b, src):
        to = lax.rem(me_d + k, nd)
        return pltpu.make_async_remote_copy(
            src_ref=out.at[:, pl.ds(pl.multiple_of(to * qrows, 8), qrows), cols_of(b)],
            dst_ref=recv.at[src, :, :, cols_of(b)],
            send_sem=dsend.at[b, k], recv_sem=drecv.at[b, src],
            device_id=(to, me_t), device_id_type=mesh_ids)

    def keep_own(b):
        mine = out[:, pl.ds(pl.multiple_of(me_d * qrows, 8), qrows), cols_of(b)]
        recv[me_d, :, :, cols_of(b)] = mine

    def brick(i, b):
        one, two = recv[i, 0, :, cols_of(b)], recv[i, 1, :, cols_of(b)]
        colors = jnp.stack([low_part(one), high_part(one), low_part(two)])
        return colors, high_part(two) * (1.0 / UNIT)

    def composite(b):
        for k in range(1, nd):
            depth_copy(k, b, lax.rem(me_d + k, nd)).wait_recv()
        color, trans = brick(0, b)
        for i in range(1, nd):
            new, new_trans = brick(i, b)
            front, back = jnp.where(ascend, color, new), jnp.where(ascend, new, color)
            color = front + jnp.where(ascend, trans, new_trans)[None] * back
            trans = trans * new_trans
        for ch in range(3):
            fin[ch, :, cols_of(b)] = coded(color[ch] + trans * (BACKDROP[ch] * UNIT))

    def tile_copy(o, part, window):
        return pltpu.make_async_remote_copy(
            src_ref=outbox.at[o, :, :, window], dst_ref=inbox.at[o, :, :, window],
            send_sem=tsend.at[part, o], recv_sem=trecv.at[part, o],
            device_id=(me_d, lax.rem(me_t + o, nt)), device_id_type=mesh_ids)

    def tile_own(part, window):
        return pltpu.make_async_copy(
            outbox.at[0, :, :, window], inbox.at[0, :, :, window], tsend.at[part, 0])

    def ship(part, window):
        def piece(p, r):
            if width == cols:
                return fin[:, pl.ds(p * rpp + r, 1), window]
            per = cols // width
            c = pl.multiple_of(lax.rem(p, per) * width, width)
            return fin[:, pl.ds(lax.div(p, per), 1), pl.ds(c, width)]

        @pl.loop(0, nt)
        def _(o):
            for r in range(rpp):
                outbox[o, :, r:r + 1, window] = join(piece(route[o, 0], r), piece(route[o, 1], r))

        tile_own(part, window).start()

        @pl.loop(1, nt)
        def _(o):
            tile_copy(o, part, window).start()

    arrive(0)
    arrive(1)
    early(0)
    arrive_halo(0)
    late(0)

    def finish(b):
        composite(b)
        if groups == nb:
            ship(b, cols_of(b))

    def block(b, beside_of):
        slot = lax.rem(b, 2)

        if isinstance(b, int):
            assert b == nb - 1
        else:
            @pl.when(b + 4 < nb)
            def _():
                dens_copy(b + 4).start()

            @pl.when(b + 2 < nb)
            def _():
                send_halo(b + 2)
                arrive(b + 2)

            arrive_halo(b + 1)

        @pl.loop(0, nd)
        def _(it):
            k = it + 1
            band = pl.multiple_of(lax.rem(me_d + k, nd) * qrows, 8)
            beside = beside_of(b + 1, 1 - slot, it)
            for part in range(parts):
                vals = march(dens16, g, slot, ascend, band, slice(part * MC, (part + 1) * MC), qrows, cells,
                             lambda step, first=part * cells: beside(first + step))
                c0, c1, c2, tr = (coded(val * UNIT) for val in vals)
                lanes = pl.ds(pl.multiple_of(b * CB + part * MC, MC), MC)
                out[0, pl.ds(band, qrows), lanes] = join(c0, c1)
                out[1, pl.ds(band, qrows), lanes] = join(c2, tr)
            beside(parts * cells)

            @pl.when(k < nd)
            def _():
                depth_copy(k, b, me_d).start()

        keep_own(b)

        @pl.when(b > 0)
        def _():
            finish(b - 1)

    def slopes_of(ahead, slot, it):
        return Beside(parts * cells, zc, lambda: across(ahead, it), lambda i: begin(ahead, it, i),
                      lambda i, dx, dyz: end(ahead, slot, it, i, dx, dyz))

    @pl.loop(0, nb - 1)
    def _(b):
        block(b, slopes_of)

    block(nb - 1, lambda ahead, slot, it: lambda step: None)
    finish(nb - 1)
    if groups != nb:
        ship(0, pl.ds(0, width))

    own_labels.wait()

    @pl.loop(1, nt)
    def _(o):
        label_copy(o).wait()

    @pl.loop(0, groups)
    def _(part):
        window = cols_of(part) if groups == nb else pl.ds(0, width)
        tile_own(part, window).wait()

        @pl.loop(1, nt)
        def _(o):
            tile_copy(o, part, window).wait()

    @pl.loop(0, nb)
    def _(b):
        for k in range(1, nd):
            depth_copy(k, b, me_d).wait_send()

    for kind in range(4):
        @pl.when(sends[kind])
        def _():
            @pl.loop(0, nb)
            def _(b):
                halo(kind, b).wait_send()


def place_kernel(arrived, inbox, display):
    nt, rpp, width = inbox.shape[0], inbox.shape[2], inbox.shape[3]
    ppd = display.shape[2]
    start = lax.axis_index("tile") * ppd

    @pl.loop(0, nt)
    def _(o):
        first, last = jnp.int32(NONE), jnp.int32(NONE)
        for p in range(ppd):
            h = arrived[o, 0, p] - start
            hit = (h >= 0) & (h < ppd)
            first = jnp.where(hit & (first == NONE), h, first)
            last = jnp.where(hit, h, last)

        def put(label, part):
            for r in range(rpp):
                piece = part(inbox[o, :, r:r + 1, :]) * (1.0 / UNIT)
                display[:, 0, pl.ds(label, 1), r * width:(r + 1) * width] = piece

        @pl.when(first != NONE)
        def _():
            put(first, low_part)

        @pl.when(last != first)
        def _():
            put(last, high_part)


def on_device(density, depth_rank, piece_home):
    cells, rows, cols = density.shape
    nd, nt = lax.axis_size("depth"), lax.axis_size("tile")
    ppd = piece_home.shape[0]
    qrows = rows // nd
    piece_len = qrows * cols // ppd
    width = min(piece_len, cols)
    rpp = piece_len // width
    nb = cols // CB
    groups = nb if width == cols else 1

    names = piece_home.reshape(1, ppd)
    left, plain, right = stencils(rows)
    anyspec = pl.BlockSpec(memory_space=pl.ANY)
    vmem = pl.BlockSpec(memory_space=pltpu.VMEM)
    smem = pl.BlockSpec(memory_space=pltpu.SMEM)
    dma = pltpu.SemaphoreType.DMA
    f32, i32 = jnp.float32, jnp.int32
    inbox, arrived = pl.pallas_call(
        lambda *refs: brick_kernel(nd, nt, ppd, *refs),
        out_shape=(jax.ShapeDtypeStruct((nt, 3, rpp, width), i32),
                   jax.ShapeDtypeStruct((nt, 1, ppd), i32)),
        in_specs=[smem, smem] + [anyspec] * 2 + [vmem] * 3,
        out_specs=(anyspec, anyspec),
        scratch_shapes=[
            pltpu.VMEM((cells + 2, rows + 2 * EDGE, cols + 2 * PAD), jnp.bfloat16),
            pltpu.VMEM((2, cells, rows, CB), f32),
            pltpu.VMEM((2, cells, rows, CB), jnp.bfloat16),
            pltpu.VMEM((2, rows, cols), i32),
            pltpu.VMEM((nd, 2, qrows, cols), i32),
            pltpu.VMEM((3, qrows, cols), i32),
            pltpu.VMEM((nt, 3, rpp, width), i32),
            pltpu.SMEM((nt, MOST), i32),
            dma((nb,)), dma((4, nb)), dma((4, nb)), dma((nb, nd)), dma((nb, nd)),
            dma((groups, nt)), dma((groups, nt)), dma((nt,)), dma((nt,)),
        ],
        compiler_params=pltpu.CompilerParams(
            collective_id=0, has_side_effects=True, vmem_limit_bytes=56 * 1024 * 1024),
    )(depth_rank, piece_home, density, names, left, plain, right)
    return pl.pallas_call(
        place_kernel,
        out_shape=jax.ShapeDtypeStruct((3, 1, ppd, piece_len), f32),
        in_specs=[smem, vmem],
        out_specs=vmem,
    )(arrived, inbox)


def solution(mesh):
    in_specs = (P("depth", "tile", None), P(), P("tile"))
    out_specs = P(None, "depth", "tile", None)
    return jax.shard_map(
        on_device, mesh=mesh, in_specs=in_specs, out_specs=out_specs, check_vma=False
    )
```

```python
import math
import jax
import jax.numpy as jnp
import numpy as np
from jax import lax
from jax.experimental import pallas as pl
from jax.experimental.pallas import tpu as pltpu
from jax.sharding import PartitionSpec as P

MOST = 2
NONE = -1

EXTINCT = 0.5
LIGHT_Z = 0.6
LIGHT_Y = 0.48
LIGHT_X = 0.64
SHARPNESS = 6.0
BACKDROP = (0.08, 0.1, 0.14)

PAD = 128
CB = 256
MC = 128
EDGE = 8
SIG_A = math.exp(-3.0)
SIG_B = math.exp(-2.5)
SHIFT = math.pi / 2 / (0.85 * math.log(2))
LEAD = 6.138231308051623e-10
SINSQ = (141379137.46788317, -4089655.3240788155, 47304.237438791075, -291.0939487912164)
UNIT = 65535.0
LOW = 65535


def stencils(rows):
    wy, wz = LIGHT_Y / LIGHT_X, LIGHT_Z / LIGHT_X
    left = np.zeros((rows, 3 * rows + 2 * EDGE), np.float32)
    for r in range(rows):
        left[r, r] = -wz
        left[r, 2 * rows + 2 * EDGE + r] = wz
        if r < rows - 1:
            left[r, rows + r + 1] = wy
        if r > 0:
            left[r, rows + r - 1] = -wy
    left[0, 2 * rows + EDGE - 1] = -wy
    left[rows - 1, 2 * rows + EDGE] = wy
    right = np.zeros((CB + 2 * PAD, CB), np.float32)
    for c in range(CB):
        right[c + PAD + 1, c] = 1.0
        right[c + PAD - 1, c] = -1.0
    plain = np.delete(left, np.s_[2 * rows:2 * rows + 2 * EDGE], axis=1)
    return [jnp.asarray(m, jnp.bfloat16) for m in (left, plain, right)]


def make_facing(d, g, dens16, left, plain, right, rows, cells, zc):
    def across(block, chunk):
        wide = d[pl.ds(chunk * zc + 1, zc), 0:rows, pl.ds(pl.multiple_of(block * CB, CB), CB + 2 * PAD)]
        wide = wide.reshape(zc * rows, CB + 2 * PAD)
        return [jnp.dot(wide[:, h:h + CB], right[h:h + CB], preferred_element_type=jnp.float32)
                for h in range(0, CB + 2 * PAD, CB)]

    def begin(block, chunk, i):
        z = chunk * zc + i
        c1 = pl.multiple_of(block * CB + PAD, PAD)
        tall = jnp.concatenate([
            d[z, 0:rows, pl.ds(c1, CB)],
            d[z + 1, :, pl.ds(c1, CB)],
            d[z + 2, 0:rows, pl.ds(c1, CB)]], axis=0)
        return jnp.dot(left[...], tall, preferred_element_type=jnp.float32)

    def end(block, slot, chunk, i, dx, dyz):
        z = chunk * zc + i
        g[slot, z] = dyz + sum(part[i * rows:(i + 1) * rows] for part in dx)
        dens16[slot, z] = d[z + 1, 0:rows, pl.ds(pl.multiple_of(block * CB + PAD, PAD), CB)]

    def inner(block, z):
        c1 = pl.multiple_of(block * CB + PAD, PAD)
        tall = d[pl.ds(z, 3), 0:rows, pl.ds(c1, CB)].reshape(3 * rows, CB)
        wide = d[z + 1, 0:rows, pl.ds(pl.multiple_of(block * CB, CB), CB + 2 * PAD)]
        dx = jnp.dot(wide, right[...], preferred_element_type=jnp.float32)
        g[0, z] = jnp.dot(plain[...], tall, preferred_element_type=jnp.float32) + dx
        dens16[0, z] = d[z + 1, 0:rows, pl.ds(c1, CB)]

    def early(block):
        @pl.loop(0, cells // 2 - 1)
        def _(i):
            for j in range(2):
                inner(block, 2 * i + 1 + j)

    def late(block):
        wy = LIGHT_Y / LIGHT_X
        c1 = pl.multiple_of(block * CB + PAD, PAD)
        for z in (0, cells - 1):
            inner(block, z)

        @pl.loop(0, cells // 4)
        def _(i):
            sub = lax.broadcasted_iota(jnp.int32, (EDGE, CB), 0)
            for j in range(4):
                z = 4 * i + j
                low = d[z + 1, rows:rows + EDGE, pl.ds(c1, CB)].astype(jnp.float32)
                high = d[z + 1, rows + EDGE:, pl.ds(c1, CB)].astype(jnp.float32)
                g[0, z, 0:EDGE] = g[0, z, 0:EDGE] - jnp.where(sub == 0, pltpu.roll(low, 1, 0), 0.0) * wy
                g[0, z, rows - EDGE:] = g[0, z, rows - EDGE:] + jnp.where(
                    sub == EDGE - 1, pltpu.roll(high, EDGE - 1, 0), 0.0) * wy

    return across, begin, end, early, late


def march(dens16, g, slot, ascend, r0, lanes, band_rows, cells, beside):
    bias = (0.35 + 0.65 * 0.5) / (0.65 * 0.5)
    zero = jnp.zeros((band_rows, MC), jnp.float32)
    trans = zero + 1.0
    total = m0 = m1 = wave = zero
    for k in range(cells):
        beside(k)
        z = jnp.where(ascend, k, cells - 1 - k)
        dens = dens16[slot, z, pl.ds(r0, band_rows), lanes].astype(jnp.float32)
        face = g[slot, z, pl.ds(r0, band_rows), lanes]
        shade = jnp.tanh(face * (0.5 * SHARPNESS * LIGHT_X)) + bias
        after = trans * jnp.exp2(dens * (-EXTINCT * math.log2(math.e)))
        ws = (trans - after) * shade
        trans = after
        v = jnp.log2(dens + 0.01) + SHIFT
        q = v * v
        c = q + SINSQ[-1]
        for coef in SINSQ[-2::-1]:
            c = c * q + coef
        c = c * q
        total = total + ws
        m0 = m0 + ws * (1.0 / (dens + (0.01 + SIG_A)))
        m1 = m1 + ws * (1.0 / (dens + (0.01 + SIG_B)))
        wave = wave + ws * (c * (1.0 / LEAD - c))
    scale = 0.65 * 0.5
    return (
        scale * (total - SIG_A * m0),
        (scale * 4 * LEAD * LEAD) * wave,
        (scale * SIG_B) * m1,
        trans,
    )


class Beside:
    def __init__(self, steps, planes, across, begin, end):
        self.across, self.begin, self.end = across, begin, end
        gap = steps // planes
        self.turns = {}
        for i in range(planes):
            self.turns.setdefault(i * gap, []).append((True, i))
            stop = min(i * gap + gap * 32 // 8, steps)
            self.turns.setdefault(stop, []).append((False, i))
        self.held, self.dx = {}, None

    def __call__(self, step):
        if step == 0:
            self.dx = self.across()
        for fresh, i in self.turns.get(step, ()):
            if fresh:
                self.held[i] = self.begin(i)
            else:
                self.end(i, self.dx, self.held[i])


def coded(value):
    return jnp.clip(value + 0.5, 0.0, UNIT).astype(jnp.int32)


def join(low, high):
    return low | (high << 16)


def low_part(word):
    return (word & LOW).astype(jnp.float32)


def high_part(word):
    return lax.shift_right_logical(word, 16).astype(jnp.float32)


def brick_kernel(nd, nt, ppd, rank, home, dens, names, left, plain, right, inbox, arrived,
                 d, g, dens16, out, recv, fin, outbox, route,
                 dens_sem, hsend, hrecv, dsend, drecv, tsend, trecv, lsend, lrecv):
    cells, rows, cols = dens.shape
    nb, parts = cols // CB, CB // MC
    zc = cells // nd
    qrows = rows // nd
    width, rpp = outbox.shape[3], outbox.shape[2]
    groups = tsend.shape[0]
    me_d, me_t = lax.axis_index("depth"), lax.axis_index("tile")
    mesh_ids = pl.DeviceIdType.MESH

    barrier = pltpu.get_barrier_semaphore()

    @pl.loop(1, nt)
    def _(o):
        pl.semaphore_signal(barrier, inc=1, device_id=(me_d, lax.rem(me_t + o, nt)), device_id_type=mesh_ids)

    for k in range(1, nd):
        pl.semaphore_signal(barrier, inc=1, device_id=(lax.rem(me_d + k, nd), me_t), device_id_type=mesh_ids)

    def cols_of(b):
        return pl.ds(pl.multiple_of(b * CB, CB), CB)

    def pads_of(b):
        return pl.ds(pl.multiple_of(b * CB + PAD, PAD), CB)

    def dens_copy(b):
        return pltpu.make_async_copy(
            dens.at[:, :, cols_of(b)], d.at[pl.ds(1, cells), pl.ds(0, rows), pads_of(b)], dens_sem.at[b])

    def halo(kind, b):
        inner = pl.ds(1, cells)
        src, dst, step = (
            (dens.at[cells - 1, :, cols_of(b)], d.at[0, pl.ds(0, rows), pads_of(b)], 1),
            (dens.at[0, :, cols_of(b)], d.at[cells + 1, pl.ds(0, rows), pads_of(b)], nd - 1),
            (dens.at[:, pl.ds(rows - EDGE, EDGE), cols_of(b)],
             d.at[inner, pl.ds(rows, EDGE), pads_of(b)], 1),
            (dens.at[:, pl.ds(0, EDGE), cols_of(b)],
             d.at[inner, pl.ds(rows + EDGE, EDGE), pads_of(b)], nt - 1),
        )[kind]
        to = (lax.rem(me_d + step, nd), me_t) if kind < 2 else (me_d, lax.rem(me_t + step, nt))
        return pltpu.make_async_remote_copy(
            src_ref=src, dst_ref=dst, send_sem=hsend.at[kind, b], recv_sem=hrecv.at[kind, b],
            device_id=to, device_id_type=mesh_ids)

    sends = (me_d < nd - 1, me_d > 0, me_t < nt - 1, me_t > 0)
    gets = (me_d > 0, me_d < nd - 1, me_t > 0, me_t < nt - 1)

    for b in range(2):
        dens_copy(b).start()

    side = jnp.zeros((cells + 2, rows + 2 * EDGE, PAD), d.dtype)
    d[:, :, :PAD] = side
    d[:, :, cols + PAD:] = side

    @pl.when(me_d == 0)
    def _():
        d[0, 0:rows, PAD:cols + PAD] = jnp.zeros((rows, cols), d.dtype)

    @pl.when(me_d == nd - 1)
    def _():
        d[cells + 1, 0:rows, PAD:cols + PAD] = jnp.zeros((rows, cols), d.dtype)

    edge = jnp.zeros((cells, EDGE, cols), d.dtype)

    @pl.when(me_t == 0)
    def _():
        d[1:cells + 1, rows:rows + EDGE, PAD:cols + PAD] = edge

    @pl.when(me_t == nt - 1)
    def _():
        d[1:cells + 1, rows + EDGE:, PAD:cols + PAD] = edge

    pl.semaphore_wait(barrier, nt - 1 + nd - 1)

    def send_halo(b):
        for kind in range(4):
            @pl.when(sends[kind])
            def _():
                halo(kind, b).start()

    send_halo(0)
    dens_copy(2).start()
    dens_copy(3).start()
    send_halo(1)

    def label_copy(o):
        return pltpu.make_async_remote_copy(
            src_ref=names, dst_ref=arrived.at[o], send_sem=lsend.at[o], recv_sem=lrecv.at[o],
            device_id=(me_d, lax.rem(me_t + o, nt)), device_id_type=mesh_ids)

    own_labels = pltpu.make_async_copy(names, arrived.at[0], lsend.at[0])
    own_labels.start()

    @pl.loop(1, nt)
    def _(o):
        label_copy(o).start()

    @pl.loop(0, nt)
    def _(o):
        start = lax.rem(me_t + o, nt) * ppd
        first, last = ppd - 1, 0
        for p in range(ppd):
            h = home[p] - start
            hit = (h >= 0) & (h < ppd)
            first = jnp.where(hit, jnp.minimum(first, p), first)
            last = jnp.where(hit, p, last)
        route[o, 0] = first
        route[o, 1] = last

    def arrive(b):
        dens_copy(b).wait()

    def arrive_halo(b):
        for kind in range(4):
            @pl.when(gets[kind])
            def _():
                halo(kind, b).wait_recv()

    ascend = rank[0] == 0
    across, begin, end, early, late = make_facing(d, g, dens16, left, plain, right, rows, cells, zc)

    def depth_copy(k, b, src):
        to = lax.rem(me_d + k, nd)
        return pltpu.make_async_remote_copy(
            src_ref=out.at[:, pl.ds(pl.multiple_of(to * qrows, 8), qrows), cols_of(b)],
            dst_ref=recv.at[src, :, :, cols_of(b)],
            send_sem=dsend.at[b, k], recv_sem=drecv.at[b, src],
            device_id=(to, me_t), device_id_type=mesh_ids)

    def keep_own(b):
        mine = out[:, pl.ds(pl.multiple_of(me_d * qrows, 8), qrows), cols_of(b)]
        recv[me_d, :, :, cols_of(b)] = mine

    def brick(i, b):
        one, two = recv[i, 0, :, cols_of(b)], recv[i, 1, :, cols_of(b)]
        colors = jnp.stack([low_part(one), high_part(one), low_part(two)])
        return colors, high_part(two) * (1.0 / UNIT)

    def composite(b):
        for k in range(1, nd):
            depth_copy(k, b, lax.rem(me_d + k, nd)).wait_recv()
        color, trans = brick(0, b)
        for i in range(1, nd):
            new, new_trans = brick(i, b)
            front, back = jnp.where(ascend, color, new), jnp.where(ascend, new, color)
            color = front + jnp.where(ascend, trans, new_trans)[None] * back
            trans = trans * new_trans
        for ch in range(3):
            fin[ch, :, cols_of(b)] = coded(color[ch] + trans * (BACKDROP[ch] * UNIT))

    def tile_copy(o, part, window):
        return pltpu.make_async_remote_copy(
            src_ref=outbox.at[o, :, :, window], dst_ref=inbox.at[o, :, :, window],
            send_sem=tsend.at[part, o], recv_sem=trecv.at[part, o],
            device_id=(me_d, lax.rem(me_t + o, nt)), device_id_type=mesh_ids)

    def tile_own(part, window):
        return pltpu.make_async_copy(
            outbox.at[0, :, :, window], inbox.at[0, :, :, window], tsend.at[part, 0])

    def ship(part, window):
        def piece(p, r):
            if width == cols:
                return fin[:, pl.ds(p * rpp + r, 1), window]
            per = cols // width
            c = pl.multiple_of(lax.rem(p, per) * width, width)
            return fin[:, pl.ds(lax.div(p, per), 1), pl.ds(c, width)]

        @pl.loop(0, nt)
        def _(o):
            for r in range(rpp):
                outbox[o, :, r:r + 1, window] = join(piece(route[o, 0], r), piece(route[o, 1], r))

        tile_own(part, window).start()

        @pl.loop(1, nt)
        def _(o):
            tile_copy(o, part, window).start()

    arrive(0)
    arrive(1)
    early(0)
    arrive_halo(0)
    late(0)

    def finish(b):
        composite(b)
        if groups == nb:
            ship(b, cols_of(b))

    def block(b, beside_of):
        slot = lax.rem(b, 2)

        if isinstance(b, int):
            assert b == nb - 1
        else:
            @pl.when(b + 4 < nb)
            def _():
                dens_copy(b + 4).start()

            @pl.when(b + 2 < nb)
            def _():
                send_halo(b + 2)
                arrive(b + 2)

            arrive_halo(b + 1)

        @pl.loop(0, nd)
        def _(it):
            k = it + 1

            @pl.when((k == nd) & (b > 0))
            def _():
                finish(b - 1)

            band = pl.multiple_of(lax.rem(me_d + k, nd) * qrows, 8)
            beside = beside_of(b + 1, 1 - slot, it)
            for part in range(parts):
                vals = march(dens16, g, slot, ascend, band, slice(part * MC, (part + 1) * MC), qrows, cells,
                             lambda step, first=part * cells: beside(first + step))
                c0, c1, c2, tr = (coded(val * UNIT) for val in vals)
                lanes = pl.ds(pl.multiple_of(b * CB + part * MC, MC), MC)
                out[0, pl.ds(band, qrows), lanes] = join(c0, c1)
                out[1, pl.ds(band, qrows), lanes] = join(c2, tr)
            beside(parts * cells)

            @pl.when(k < nd)
            def _():
                depth_copy(k, b, me_d).start()

        keep_own(b)

    def slopes_of(ahead, slot, it):
        return Beside(parts * cells, zc, lambda: across(ahead, it), lambda i: begin(ahead, it, i),
                      lambda i, dx, dyz: end(ahead, slot, it, i, dx, dyz))

    @pl.loop(0, nb - 1)
    def _(b):
        block(b, slopes_of)

    block(nb - 1, lambda ahead, slot, it: lambda step: None)
    finish(nb - 1)
    if groups != nb:
        ship(0, pl.ds(0, width))

    own_labels.wait()

    @pl.loop(1, nt)
    def _(o):
        label_copy(o).wait()

    @pl.loop(0, groups)
    def _(part):
        window = cols_of(part) if groups == nb else pl.ds(0, width)
        tile_own(part, window).wait()

        @pl.loop(1, nt)
        def _(o):
            tile_copy(o, part, window).wait()

    @pl.loop(0, nb)
    def _(b):
        for k in range(1, nd):
            depth_copy(k, b, me_d).wait_send()

    for kind in range(4):
        @pl.when(sends[kind])
        def _():
            @pl.loop(0, nb)
            def _(b):
                halo(kind, b).wait_send()


def place_kernel(arrived, inbox, display):
    nt, rpp, width = inbox.shape[0], inbox.shape[2], inbox.shape[3]
    ppd = display.shape[2]
    start = lax.axis_index("tile") * ppd

    @pl.loop(0, nt)
    def _(o):
        first, last = jnp.int32(NONE), jnp.int32(NONE)
        for p in range(ppd):
            h = arrived[o, 0, p] - start
            hit = (h >= 0) & (h < ppd)
            first = jnp.where(hit & (first == NONE), h, first)
            last = jnp.where(hit, h, last)

        def put(label, part):
            for r in range(rpp):
                piece = part(inbox[o, :, r:r + 1, :]) * (1.0 / UNIT)
                display[:, 0, pl.ds(label, 1), r * width:(r + 1) * width] = piece

        @pl.when(first != NONE)
        def _():
            put(first, low_part)

        @pl.when(last != first)
        def _():
            put(last, high_part)


def on_device(density, depth_rank, piece_home):
    cells, rows, cols = density.shape
    nd, nt = lax.axis_size("depth"), lax.axis_size("tile")
    ppd = piece_home.shape[0]
    qrows = rows // nd
    piece_len = qrows * cols // ppd
    width = min(piece_len, cols)
    rpp = piece_len // width
    nb = cols // CB
    groups = nb if width == cols else 1

    names = piece_home.reshape(1, ppd)
    left, plain, right = stencils(rows)
    anyspec = pl.BlockSpec(memory_space=pl.ANY)
    vmem = pl.BlockSpec(memory_space=pltpu.VMEM)
    smem = pl.BlockSpec(memory_space=pltpu.SMEM)
    dma = pltpu.SemaphoreType.DMA
    f32, i32 = jnp.float32, jnp.int32
    inbox, arrived = pl.pallas_call(
        lambda *refs: brick_kernel(nd, nt, ppd, *refs),
        out_shape=(jax.ShapeDtypeStruct((nt, 3, rpp, width), i32),
                   jax.ShapeDtypeStruct((nt, 1, ppd), i32)),
        in_specs=[smem, smem] + [anyspec] * 2 + [vmem] * 3,
        out_specs=(anyspec, anyspec),
        scratch_shapes=[
            pltpu.VMEM((cells + 2, rows + 2 * EDGE, cols + 2 * PAD), jnp.bfloat16),
            pltpu.VMEM((2, cells, rows, CB), f32),
            pltpu.VMEM((2, cells, rows, CB), jnp.bfloat16),
            pltpu.VMEM((2, rows, cols), i32),
            pltpu.VMEM((nd, 2, qrows, cols), i32),
            pltpu.VMEM((3, qrows, cols), i32),
            pltpu.VMEM((nt, 3, rpp, width), i32),
            pltpu.SMEM((nt, MOST), i32),
            dma((nb,)), dma((4, nb)), dma((4, nb)), dma((nb, nd)), dma((nb, nd)),
            dma((groups, nt)), dma((groups, nt)), dma((nt,)), dma((nt,)),
        ],
        compiler_params=pltpu.CompilerParams(
            collective_id=0, has_side_effects=True, vmem_limit_bytes=56 * 1024 * 1024),
    )(depth_rank, piece_home, density, names, left, plain, right)
    return pl.pallas_call(
        place_kernel,
        out_shape=jax.ShapeDtypeStruct((3, 1, ppd, piece_len), f32),
        in_specs=[smem, vmem],
        out_specs=vmem,
    )(arrived, inbox)


def solution(mesh):
    in_specs = (P("depth", "tile", None), P(), P("tile"))
    out_specs = P(None, "depth", "tile", None)
    return jax.shard_map(
        on_device, mesh=mesh, in_specs=in_specs, out_specs=out_specs, check_vma=False
    )
```
